256 devices in a mesh: pool: 64 (over z, x, core), rep: 4 (over y).
Axes of the slice: x: 4, y: 4, z: 8, core: 2. Of those that a mesh axis runs over, the one named last changes fastest.
Arguments:
- query_vecs: bfloat16 [4096, 32, 128], P(('pool', 'rep')), may hold values from -0.5 to 0.5
- passage_vecs: bfloat16 [2048, 256, 128], P('pool'), may hold values from -0.5 to 0.5
- owner_ids: int32 [4096, 4], P(('pool', 'rep')), may hold values from 0 to 63, all different within a row; in each aligned block of 16 rows (0 to 15, 16 to 31, ...) at most 2 rows name the same one
- local_ids: int32 [4096, 4, 4], P(('pool', 'rep')), may hold values from 0 to 31
- cand_mask: int32 [4096, 16], P(('pool', 'rep')), may hold values 0 or 1
Outputs:
- query_loss: float32 [4096], P(('pool', 'rep'))
- grad_query: float32 [4096, 32, 128], P(('pool', 'rep'))
- grad_passage: float32 [2048, 256, 128], P('pool', 'rep')
The draws below stay inside these ranges and needn't reach their ends.
Inputs may be any that keep to these rules, and one draw needn't show every extreme that they name: `owner_ids`: each row names 4 different pool shards. Among the 16 rows of one device no shard is named more than 2 times, and in some devices' rows one shard is named exactly 2 times.
All inputs are finite; a program needn't handle non-finite values. No bound on the sum of `cand_mask` on one device may be relied on, other than what follows from the above.
Results may differ from the reference program's by a relative error of at most 0.014.
Values may be sent and summed in bfloat16 or wider, within the bound.
A program may use at most 128 MiB of HBM per device.

```python
import math
import jax
import jax.numpy as jnp
import numpy as np
from jax import lax

DIM = 128
QTOK = 32
PTOK = 256
GROUPS = 4
PER_GROUP = 4
CANDS = 16
QRY_DEV = 16
PASS_DEV = 32
CAP = 2
QUERIES = 4096
PASSAGES = 2048
N_POOL = 64


def touch_ends(entries, key, least, high):
    longest = entries.shape.index(max(entries.shape))
    spots = []
    for shift in (0, 1):
        where = [jax.random.randint(jax.random.fold_in(key, axis), (), 0, length) for axis, length in enumerate(entries.shape)]
        where[longest] = (where[longest] + shift) % entries.shape[longest]
        spots.append(tuple(where))
    return entries.at[spots[0]].set(least).at[spots[1]].set(high)


def block_scale(rng, shape, shards, least, high):
    loudness = 1.0
    for position, shards_of in shards:
        draws = jax.random.uniform(jax.random.fold_in(jax.random.fold_in(rng, 6), position), (shards_of,), jnp.float32, least / len(shards), high / len(shards))
        loudness = loudness * jnp.repeat(jnp.exp(draws), shape[position] // shards_of).reshape((-1,) + (1,) * (len(shape) - 1 - position))
    return loudness


def assign_block(own_key, own, number, rows, amount, top, bound, lean):
    order = jax.random.permutation(own_key, amount)
    packed, common = portions_of(amount, rows * top, bound, lean, True), portions_of(amount, rows * top, bound, lean, False)
    places = jnp.arange(amount)

    def named(tallies, offset_by):
        used = int((tallies > 0).sum())
        fixed = max(1, used // 4)
        passed = fixed + (places - fixed + offset_by * (used - fixed)) % max(1, amount - fixed)
        return jnp.zeros((amount,), jnp.int32).at[order[jnp.where(places < fixed, places, passed)]].set(jnp.asarray(tallies, jnp.int32))

    tallies = jnp.where(number % 4 == 0, named(packed, number // 4), named(common, number - number // 4 - 1))
    mixed = jax.random.permutation(jax.random.fold_in(own, 3), amount)
    source_of, taker = mixed[0:amount // 2 * 2:2], mixed[1:amount // 2 * 2:2]
    room = jnp.minimum(tallies[source_of] - 1, bound - tallies[taker]) // 2
    room = jnp.where((source_of == order[0]) | (taker == order[0]) | (tallies[taker] == 0), 0, jnp.maximum(room, 0))
    passed = jax.random.randint(jax.random.fold_in(own, 4), (amount // 2,), 0, 1 << 20) % (room + 1)
    tallies = tallies.at[source_of].add(-passed).at[taker].add(passed)
    members = jnp.searchsorted(jnp.cumsum(tallies), jnp.arange(rows * top), side="right").astype(jnp.int32)
    table = members.reshape(top, rows).T
    table = table[jax.random.permutation(jax.random.fold_in(own, 1), rows)]
    offset_by = jax.random.randint(jax.random.fold_in(own, 2), (rows, 1), 0, top)
    return jnp.take_along_axis(table, (jnp.arange(top)[None, :] + offset_by) % top, axis=1)


def portions_of(count, total, most, slope, full):
    loads = [(1 << 20) // math.isqrt(standing ** slope) + 1 for standing in range(1, count + 1)]
    largest = most if full else min(most, max(-(-total // count), total * loads[0] // sum(loads)))
    least = 1 if total - largest >= count - 1 else 0
    counts, rest = [largest] + [least] * (count - 1), total - largest - least * (count - 1)
    while rest > 0:
        free = [i for i in range(1, count) if counts[i] < largest] or [i for i in range(1, count) if counts[i] < most]
        whole, budget = sum([loads[i] for i in free]), rest
        for i in free:
            addition = min(most - counts[i], max(1, budget * loads[i] // whole), rest)
            counts[i] = counts[i] + addition
            rest = rest - addition
    return np.array(counts)


def centred(own_key, shape, spread, reach, pieces=(), dtype=jnp.bfloat16):
    level = block_scale(own_key, shape, pieces, -0.22, 0.18) if pieces else 1.0
    entries = jax.random.normal(own_key, shape, jnp.float32) * spread * level
    return jnp.minimum(jnp.maximum(entries, -reach), reach).astype(dtype)


def setup_inputs(seed: int = 0) -> dict:
    splits = jax.random.split(jax.random.key(seed), 6)
    query_vecs = centred(splits[0], (QUERIES, QTOK, DIM), 0.0884, 0.5, ((0, 256),))
    passage_vecs = centred(splits[1], (PASSAGES, PTOK, DIM), 0.0884, 0.5, ((0, 64),))
    owner_ids_keys = jax.random.split(jax.random.fold_in(splits[2], 1), QUERIES // QRY_DEV)
    owner_ids_turns = jax.random.permutation(jax.random.fold_in(splits[2], 3), QUERIES // QRY_DEV)
    owner_ids = jax.vmap(lambda own, number: assign_block(jax.random.fold_in(splits[2], 2), own, number, QRY_DEV, N_POOL, GROUPS, CAP, 2))(owner_ids_keys, owner_ids_turns).reshape((QUERIES, GROUPS))
    local_ids = touch_ends(jax.random.randint(splits[3], (QUERIES, GROUPS, PER_GROUP), 0, PASS_DEV), jax.random.fold_in(splits[3], 1), 0, PASS_DEV - 1).astype(jnp.int32)
    cand_mask = touch_ends((jax.random.randint(splits[4], (QUERIES, CANDS), 0, 4) < 3).astype(jnp.int32), jax.random.fold_in(splits[4], 1), 0, 1)
    return dict(query_vecs=query_vecs, passage_vecs=passage_vecs, owner_ids=owner_ids, local_ids=local_ids, cand_mask=cand_mask)


temper = 0.05
loss_scale = 16.0
epsilon = 1e-06

def normalize(vectors):
    widened = vectors.astype(jnp.float32)
    inverse = lax.rsqrt(lax.optimization_barrier(jnp.sum(widened * widened, axis=-1, keepdims=True)) + epsilon)
    return (widened * inverse, inverse)

def unit_backward(unit_vecs, inverse, upstream):
    return inverse * (upstream - unit_vecs * lax.optimization_barrier(jnp.sum(unit_vecs * upstream, axis=-1, keepdims=True)))

def reference(query_vecs, passage_vecs, owner_ids, local_ids, cand_mask):
    q_unit, q_inverse = normalize(query_vecs)
    p_unit, p_inverse = normalize(passage_vecs)
    q_low = q_unit.astype(jnp.bfloat16)
    p_low = p_unit.astype(jnp.bfloat16)
    passage_ids = (owner_ids[:, :, None] * PASS_DEV + local_ids).reshape(QUERIES, CANDS).astype(jnp.int32)
    is_first = jnp.arange(CANDS) == 0
    valid_flags = jnp.maximum(cand_mask, is_first.astype(jnp.int32))
    block_rows = 32 if QUERIES % 32 == 0 else 1
    block_count = QUERIES // block_rows

    def one_block(accumulated, block_input):
        queries, cand_rows, valid_block = block_input
        candidates = p_low[cand_rows]
        sim_scores = jnp.einsum('bid,bckd->bcik', queries.astype(jnp.float32), candidates.astype(jnp.float32))
        log_sums = jnp.log(lax.optimization_barrier(jnp.sum(jnp.exp(sim_scores / temper), axis=-1)))
        scores = temper * lax.optimization_barrier(jnp.sum(log_sums, axis=-1))
        exp_terms = jnp.exp(scores) * valid_block.astype(jnp.float32)
        denominator = lax.optimization_barrier(jnp.sum(exp_terms, axis=-1, keepdims=True))
        losses = jnp.log(denominator[:, 0]) - scores[:, 0]
        dscore = loss_scale * (exp_terms / denominator - is_first.astype(jnp.float32))
        dsoft = (dscore[:, :, None, None] * jnp.exp(sim_scores / temper - log_sums[..., None])).astype(jnp.bfloat16)
        dsoft_wide = dsoft.astype(jnp.float32)
        grouped_soft = dsoft_wide.reshape(block_rows, GROUPS, PER_GROUP, QTOK, PTOK)
        grouped_cands = candidates.astype(jnp.float32).reshape(block_rows, GROUPS, PER_GROUP, PTOK, DIM)
        group_part = jnp.einsum('bgjik,bgjkd->bgid', grouped_soft, grouped_cands).astype(jnp.bfloat16)
        query_grad = lax.optimization_barrier(jnp.sum(group_part.astype(jnp.float32), axis=1))
        passage_grad = jnp.einsum('bcik,bid->bckd', dsoft_wide, queries.astype(jnp.float32))
        accumulated = accumulated.at[cand_rows.reshape(-1)].add(passage_grad.reshape(-1, PTOK, DIM))
        return (accumulated, (losses, query_grad))
    start_grad = jnp.zeros((PASSAGES, PTOK, DIM), jnp.float32)
    inputs = (q_low.reshape(block_count, block_rows, QTOK, DIM), passage_ids.reshape(block_count, block_rows, CANDS), valid_flags.reshape(block_count, block_rows, CANDS))
    g_passage, (losses, g_query) = lax.scan(one_block, start_grad, inputs)
    g_query = g_query.reshape(QUERIES, QTOK, DIM)
    grad_query = unit_backward(q_unit, q_inverse, g_query)
    grad_passage = unit_backward(p_unit, p_inverse, g_passage)
    return (losses.reshape(QUERIES), grad_query, grad_passage)
```

```python
import math

import jax
import jax.numpy as jnp
from jax import lax
from jax.experimental import pallas as pl
from jax.experimental.pallas import tpu as pltpu
from jax.sharding import PartitionSpec as P

MESH = pl.DeviceIdType.MESH
f32, bf16, i32 = jnp.float32, jnp.bfloat16, jnp.int32

TEMPER = 0.05
LOSS_SCALE = 16.0
EPSILON = 1e-06

NP = 64
NR = 4
CAP = 2
NQ = 16
QT = 32
DIM = 128
PT = 256
NPASS = 32
GROUPS = 4
WIDTH = 4
SLOTS = NP * CAP
TILE = 8
NTILES = (SLOTS * WIDTH + NPASS * (TILE - 1)) // TILE
SHARE = PT // NR
RS_CHUNK = 8
HIGH = lax.Precision.HIGHEST


def iota(shape, dim):
    return lax.broadcasted_iota(i32, shape, dim)


def hot(cond, dtype=f32):
    return jnp.where(cond, 1.0, 0.0).astype(dtype)


def index(x, bound):
    return jnp.clip(x.astype(i32), 0, bound - 1)


def dot(a, b):
    return jnp.dot(a.astype(bf16), b.astype(bf16), preferred_element_type=f32)


def dot_nt(a, b):
    return lax.dot_general(
        a.astype(bf16), b.astype(bf16), (((1,), (1,)), ((), ())), preferred_element_type=f32
    )


def hdot(a, b):
    return jnp.dot(a, b, preferred_element_type=f32, precision=HIGH)


def hdot_nt(a, b):
    return lax.dot_general(
        a, b, (((1,), (1,)), ((), ())), preferred_element_type=f32, precision=HIGH
    )


def kernel(
    q_ref, p_any, meta_ref,
    loss_ref, gq_ref, gp_ref,
    p_raw, p_low, q_low, q_send, q_recv, meta_send, meta_recv, sc_send, sc_recv, w_send, w_recv,
    rows_ref, rhs_ref, soft_ref, a_ref, qn_ref, ret_send, ret_recv, rs_send, rs_recv,
    tbla_v, tblb_v, wt_v, tbla, tblb, wt,
    sem_p, sem_tbl, q_ss, q_rs, m_ss, m_rs, s_ss, s_rs, w_ss, w_rs, r_ss, r_rs, x_ss, x_rs,
):
    me = lax.axis_index("pool")
    rep = lax.axis_index("rep")

    def wait_bytes(ref, sem):
        pltpu.make_async_copy(ref, ref, sem).wait()

    def to_pool(src, dst, ss, rs, peer):
        return pltpu.make_async_remote_copy(
            src_ref=src, dst_ref=dst, send_sem=ss, recv_sem=rs, device_id=(peer, rep), device_id_type=MESH
        )

    p_copy = pltpu.make_async_copy(p_any, p_raw, sem_p)
    p_copy.start()

    barrier = pltpu.get_barrier_semaphore()

    def greet(d, _):
        pl.semaphore_signal(
            barrier, inc=1, device_id=(lax.rem(me + d, NP), rep), device_id_type=MESH
        )
        return 0

    lax.fori_loop(1, NP, greet, 0)
    for d in range(1, NR):
        pl.semaphore_signal(
            barrier, inc=1, device_id=(me, lax.rem(rep + d, NR)), device_id_type=MESH
        )

    for a in range(NQ):
        x = q_ref[a].astype(f32)
        inv = lax.rsqrt(jnp.sum(x * x, axis=-1, keepdims=True) + EPSILON)
        q_low[a] = (x * inv).astype(bf16)

    npair = GROUPS * NQ
    mf = meta_ref[...].astype(f32)
    cols = mf.shape[1]
    lane_m = iota((NQ, cols), 1)
    own_col = jnp.concatenate(
        [
            jnp.sum(jnp.where(lane_m == g, mf, 0.0), axis=1, keepdims=True)
            for g in range(GROUPS)
        ],
        axis=0,
    )
    src_r, dst_c = iota((cols, 128), 0), iota((cols, 128), 1)
    loc_w = jnp.concatenate(
        [
            dot(mf, hot((src_r == GROUPS + WIDTH * g + dst_c) & (dst_c < WIDTH)))
            for g in range(GROUPS)
        ],
        axis=0,
    )
    mask_w = [
        dot(mf, hot((src_r == GROUPS + GROUPS * WIDTH + WIDTH * g + dst_c) & (dst_c < WIDTH)))
        for g in range(GROUPS)
    ]
    ra, ca = iota((npair, npair), 0), iota((npair, npair), 1)
    own_row = jnp.sum(jnp.where(ra == ca, own_col, 0.0), axis=0, keepdims=True)
    same = own_col == own_row
    rank_col = jnp.sum(hot(same & (ca % NQ < ra % NQ)), axis=1, keepdims=True)
    rank_row = jnp.sum(hot(same & (ra % NQ < ca % NQ)), axis=0, keepdims=True)
    slot_col = CAP * own_col + rank_col
    slot_row = CAP * own_row + rank_row
    st = hot(slot_col == iota((npair, SLOTS), 1).astype(f32))
    s_hot = hot(slot_row == iota((SLOTS, npair), 0).astype(f32))
    qidx_row = jnp.sum(
        st * (iota((npair, SLOTS), 0) % NQ).astype(f32), axis=0, keepdims=True
    )
    slot_wide = jnp.sum(
        jnp.where(iota((npair, 128), 0) == iota((npair, 128), 1), slot_col, 0.0),
        axis=0, keepdims=True,
    )
    tbla_v[0:8, :] = index(jnp.broadcast_to(qidx_row, (8, 128)), NQ)
    tbla_v[8:16, :] = index(jnp.broadcast_to(slot_wide, (8, 128)), SLOTS)
    tbla_copy = pltpu.make_async_copy(tbla_v, tbla, sem_tbl)
    tbla_copy.start()
    loc_slots = dot(s_hot, loc_w)
    for peer in range(NP):
        meta_send[peer] = loc_slots[CAP * peer : CAP * (peer + 1), :]
    tbla_copy.wait()
    pl.semaphore_wait(barrier, NP - 1 + NR - 1)

    def send_meta(d, _):
        peer = lax.rem(me + d, NP)
        to_pool(meta_send.at[peer], meta_recv.at[me], m_ss, m_rs, peer).start()
        return 0

    lax.fori_loop(1, NP, send_meta, 0)
    meta_recv[me] = meta_send[me]

    def send_q(d, _):
        peer = lax.rem(me + d, NP)
        for k in range(CAP):
            q_send[CAP * peer + k] = q_low[tbla[0, CAP * peer + k]]
        to_pool(
            q_send.at[pl.ds(CAP * peer, CAP)], q_recv.at[pl.ds(CAP * me, CAP)], q_ss, q_rs, peer
        ).start()
        return 0

    lax.fori_loop(1, NP, send_q, 0)
    for k in range(CAP):
        q_recv[CAP * me + k] = q_low[tbla[0, CAP * me + k]]

    p_copy.wait()

    def norm_passage(p, _):
        x = p_raw[p].astype(f32)
        inv = lax.rsqrt(jnp.sum(x * x, axis=-1, keepdims=True) + EPSILON)
        p_low[p] = (x * inv).astype(bf16)
        return 0

    lax.fori_loop(0, NPASS, norm_passage, 0)

    wait_bytes(meta_recv.at[pl.ds(0, NP - 1)], m_rs)
    for peer in range(NP):
        rows_ref[CAP * peer : CAP * (peer + 1), :] = meta_recv[peer]
    loc_r = rows_ref[...]
    r_i, c_i = iota((128, 128), 0), iota((128, 128), 1)
    pc, jc, pr, jr = c_i % NPASS, c_i // NPASS, r_i % NPASS, r_i // NPASS
    one_hot = hot(dot(loc_r, hot((r_i == jc) & (r_i < WIDTH))) == pc.astype(f32))
    before = dot(hot(c_i < r_i), one_hot)
    total = jnp.broadcast_to(jnp.sum(one_hot, axis=0, keepdims=True), (8, 128))
    base = dot(total, hot((pr == pc) & (jr < jc)))[0:1, :]
    tiles = jnp.floor((dot(total, hot(pr == pc)) + (TILE - 1)) * (1.0 / TILE))
    offset = dot(tiles, hot((jr == 0) & (pr < pc)))
    rank = base + before
    rank_tile = jnp.floor(rank * (1.0 / TILE))
    x_tile = one_hot * (offset[0:1, :] + rank_tile)
    x_rest = one_hot * (rank - TILE * rank_tile)
    fold = hot((c_i == jr) & (c_i < WIDTH))
    tile_c = dot(x_tile, fold)
    rest_c = dot(x_rest, fold)
    fold_row = hot(iota((8, 128), 0) == iota((8, 128), 1) // NPASS)
    tile_r = dot_nt(fold_row, x_tile)
    rest_r = dot_nt(fold_row, x_rest)
    loc_rows = dot_nt(hot(iota((8, 128), 0) == iota((8, 128), 1)), loc_r)
    sub8 = iota((8, 128), 0).astype(f32)
    slot_ids = iota((8, 128), 1).astype(f32)
    table = jnp.zeros((16, 128), f32)
    for j in range(WIDTH):
        rest_j = rest_r[j : j + 1, :]
        lhs = jnp.concatenate(
            [
                jnp.where(rest_j == sub8, slot_ids, 0.0),
                jnp.where(rest_j == 0.0, loc_rows[j : j + 1, :], jnp.zeros((8, 128), f32)),
            ],
            axis=0,
        )
        rhs = hot(tile_c[:, j : j + 1] == c_i.astype(f32))
        rhs_ref[j] = rhs
        table = table + dot(lhs, rhs)
    tblb_v[0:8, :] = index(table[0:8], SLOTS)
    tblb_v[8:16, :] = index(table[8:16], NPASS)
    tblb_v[16:24, :] = index(TILE * tile_r + rest_r, NTILES * TILE)
    tblb_v[24:32, :] = index(offset + tiles - 1.0, NTILES)
    tblb_v[32:40, :] = index(tiles, 2)
    tblb_copy = pltpu.make_async_copy(tblb_v, tblb, sem_tbl)
    tblb_copy.start()
    tblb_copy.wait()

    wait_bytes(q_recv.at[pl.ds(0, CAP * (NP - 1))], q_rs)
    ones = jnp.ones((PT, DIM), bf16)
    lane8 = iota((8, 128), 1)

    def forward_tile(t, scores):
        p_tile = p_low[tblb[8, t]]
        q_tile = jnp.concatenate([q_recv[tblb[r, t]] for r in range(TILE)], axis=0)
        sims = lax.dot_general(
            q_tile, p_tile, (((1,), (1,)), ((), ())), preferred_element_type=f32
        )
        soft = jnp.exp2(sims * (math.log2(math.e) / TEMPER)).astype(bf16)
        soft_ref[t] = soft
        both = jnp.dot(
            soft, jnp.concatenate([p_tile, ones], axis=1), preferred_element_type=f32
        )
        sums = both[:, DIM:]
        inv = 1.0 / sums
        a_ref[pl.ds(TILE * t, TILE)] = (both[:, :DIM] * inv).reshape(TILE, QT, DIM)
        qn_ref[t] = q_tile.astype(f32) * inv
        means = (sums * (1.0 / PT)).reshape(TILE, QT // 8, 8, DIM)
        product = means[:, 0]
        for i in range(1, QT // 8):
            product = product * means[:, i]
        logs = jnp.sum(jnp.log(product), axis=1)
        score = TEMPER * (logs + QT * math.log(PT))
        return jnp.where(lane8 == t, score, scores)

    scores = lax.fori_loop(0, NTILES, forward_tile, jnp.zeros((8, 128), f32))

    sc = jnp.zeros((SLOTS, 128), f32)
    lane_s = iota((SLOTS, 128), 1)
    lane_r = iota((SLOTS, 8), 1).astype(f32)
    for j in range(WIDTH):
        picked = hdot_nt(rhs_ref[j], scores)
        col = jnp.sum(
            jnp.where(rest_c[:, j : j + 1] == lane_r, picked, 0.0), axis=1, keepdims=True
        )
        sc = jnp.where(lane_s == j, col, sc)
    for peer in range(NP):
        sc_send[peer] = sc[CAP * peer : CAP * (peer + 1), :]

    def send_sc(d, _):
        peer = lax.rem(me + d, NP)
        to_pool(sc_send.at[peer], sc_recv.at[me], s_ss, s_rs, peer).start()
        return 0

    lax.fori_loop(1, NP, send_sc, 0)
    sc_recv[me] = sc_send[me]
    wait_bytes(sc_recv.at[pl.ds(0, NP - 1)], s_rs)
    for peer in range(NP):
        rows_ref[CAP * peer : CAP * (peer + 1), :] = sc_recv[peer]

    own_scores = hdot(st, rows_ref[...])
    lane_q = iota((NQ, 128), 1)
    denom = jnp.zeros((NQ, 1), f32)
    exps = []
    for g in range(GROUPS):
        valid = mask_w[g]
        if g == 0:
            valid = jnp.where(lane_q == 0, 1.0, valid)
        e = jnp.exp(own_scores[NQ * g : NQ * (g + 1), :]) * valid
        exps.append(e)
        denom = denom + jnp.sum(e, axis=1, keepdims=True)
    losses = jnp.log(denom) - own_scores[0:NQ, 0:1]
    loss_ref[...] = jnp.sum(
        jnp.where(iota((NQ, NQ), 0) == iota((NQ, NQ), 1), losses, 0.0), axis=0, keepdims=True
    )
    dscore = [LOSS_SCALE * (e / denom) for e in exps]
    dscore[0] = dscore[0] - jnp.where(lane_q == 0, LOSS_SCALE, 0.0)
    w_slots = hdot(s_hot, jnp.concatenate(dscore, axis=0))
    for peer in range(NP):
        w_send[peer] = w_slots[CAP * peer : CAP * (peer + 1), :]

    def send_w(d, _):
        peer = lax.rem(me + d, NP)
        to_pool(w_send.at[peer], w_recv.at[me], w_ss, w_rs, peer).start()
        return 0

    lax.fori_loop(1, NP, send_w, 0)
    w_recv[me] = w_send[me]
    wait_bytes(w_recv.at[pl.ds(0, NP - 1)], w_rs)
    for peer in range(NP):
        rows_ref[CAP * peer : CAP * (peer + 1), :] = w_recv[peer]

    w_rows = hdot_nt(hot(iota((8, 128), 0) == iota((8, 128), 1)), rows_ref[...])
    w_tile = jnp.zeros((8, 128), f32)
    for j in range(WIDTH):
        lhs = jnp.where(rest_r[j : j + 1, :] == sub8, w_rows[j : j + 1, :], 0.0)
        w_tile = w_tile + hdot(lhs, rhs_ref[j])
    wt_v[...] = w_tile
    wt_copy = pltpu.make_async_copy(wt_v, wt, sem_tbl)
    wt_copy.start()
    wt_copy.wait()

    def group_grad(s):
        acc = jnp.zeros((QT, DIM), f32)
        for j in range(WIDTH):
            pos = tblb[16 + j, s]
            acc = acc + wt[pos & (TILE - 1), pos >> 3] * a_ref[pos]
        return acc.astype(bf16)

    def send_ret(d, _):
        peer = lax.rem(me + d, NP)
        for k in range(CAP):
            ret_send[CAP * peer + k] = group_grad(CAP * peer + k)
        to_pool(
            ret_send.at[pl.ds(CAP * peer, CAP)], ret_recv.at[pl.ds(CAP * me, CAP)], r_ss, r_rs, peer
        ).start()
        return 0

    lax.fori_loop(1, NP, send_ret, 0)
    for k in range(CAP):
        ret_recv[CAP * me + k] = group_grad(CAP * me + k)

    def passage_tile(t, _):
        qs = jnp.concatenate(
            [
                (qn_ref[t, QT * r : QT * (r + 1), :] * wt[r, t]).astype(bf16)
                for r in range(TILE)
            ],
            axis=0,
        )
        grad = lax.dot_general(
            qs, soft_ref[t], (((0,), (0,)), ((), ())), preferred_element_type=f32
        )
        halves = jnp.concatenate([grad[:, :128], grad[:, 128:]], axis=0).reshape(TILE, QT, DIM)
        prev = jnp.maximum(t - 1, 0)
        again = (t > 0) & (tblb[8, t] == tblb[8, prev])
        keep = jnp.where(again, 1.0, 0.0).astype(f32)
        a_ref[pl.ds(TILE * t, TILE)] = halves + keep * a_ref[pl.ds(TILE * prev, TILE)]
        return 0

    lax.fori_loop(0, NTILES, passage_tile, 0)

    for chunk in range(NPASS // RS_CHUNK):

        def cut_passage(i, _):
            p = chunk * RS_CHUNK + i
            last = TILE * tblb[24, p]
            used = tblb[32, p].astype(f32)
            for half in range(2):
                x = jnp.concatenate(
                    [a_ref[last + 4 * half + m] for m in range(4)], axis=0
                )
                y = (x * used).T.astype(bf16)
                for part in range(2):
                    rs_send[2 * half + part, p] = y[SHARE * part : SHARE * (part + 1), :]
            return 0

        lax.fori_loop(0, RS_CHUNK, cut_passage, 0)
        rows = pl.ds(chunk * RS_CHUNK, RS_CHUNK)
        for d in range(1, NR):
            target = lax.rem(rep + d, NR)
            pltpu.make_async_remote_copy(
                src_ref=rs_send.at[target, rows],
                dst_ref=rs_recv.at[d - 1, rows],
                send_sem=x_ss,
                recv_sem=x_rs,
                device_id=(me, target),
                device_id_type=MESH,
            ).start()

    wait_bytes(ret_recv.at[pl.ds(0, CAP * (NP - 1))], r_rs)

    def finish_query(a, _):
        x = q_ref[a].astype(f32)
        inv = lax.rsqrt(jnp.sum(x * x, axis=-1, keepdims=True) + EPSILON)
        unit = x * inv
        up = jnp.zeros((QT, DIM), f32)
        for g in range(GROUPS):
            up = up + ret_recv[tbla[8, NQ * g + a]].astype(f32)
        gq_ref[a] = inv * (up - unit * jnp.sum(unit * up, axis=-1, keepdims=True))
        return 0

    lax.fori_loop(0, NQ, finish_query, 0)

    wait_bytes(rs_recv, x_rs)
    start = pl.multiple_of(rep * SHARE, SHARE)

    def finish_passage(p, _):
        x = p_raw[p, pl.ds(start, SHARE), :].astype(f32)
        inv = lax.rsqrt(jnp.sum(x * x, axis=-1, keepdims=True) + EPSILON)
        unit = x * inv
        up = rs_send[rep, p].astype(f32)
        for d in range(NR - 1):
            up = up + rs_recv[d, p].astype(f32)
        gp_ref[p] = inv * (up - unit * jnp.sum(unit * up, axis=-1, keepdims=True))
        return 0

    lax.fori_loop(0, NPASS, finish_passage, 0)

    wait_bytes(meta_send.at[pl.ds(0, NP - 1)], m_ss)
    wait_bytes(q_send.at[pl.ds(0, CAP * (NP - 1))], q_ss)
    wait_bytes(sc_send.at[pl.ds(0, NP - 1)], s_ss)
    wait_bytes(w_send.at[pl.ds(0, NP - 1)], w_ss)
    wait_bytes(ret_send.at[pl.ds(0, CAP * (NP - 1))], r_ss)
    wait_bytes(rs_recv, x_ss)


def per_device(query_vecs, passage_vecs, owner_ids, local_ids, cand_mask):
    meta = jnp.concatenate(
        [owner_ids, local_ids.reshape(NQ, GROUPS * WIDTH), cand_mask], axis=1
    )
    vmem = pl.BlockSpec(memory_space=pltpu.VMEM)
    rows = pltpu.VMEM((NP, CAP, 128), f32)
    dma = pltpu.SemaphoreType.DMA
    loss, grad_query, grad_passage = pl.pallas_call(
        kernel,
        out_shape=(
            jax.ShapeDtypeStruct((1, NQ), f32),
            jax.ShapeDtypeStruct((NQ, QT, DIM), f32),
            jax.ShapeDtypeStruct((NPASS, SHARE, DIM), f32),
        ),
        in_specs=[vmem, pl.BlockSpec(memory_space=pl.ANY), vmem],
        out_specs=[vmem, vmem, vmem],
        scratch_shapes=[
            pltpu.VMEM((NPASS, PT, DIM), bf16),
            pltpu.VMEM((NPASS, PT, DIM), bf16),
            pltpu.VMEM((NQ, QT, DIM), bf16),
            pltpu.VMEM((SLOTS, QT, DIM), bf16),
            pltpu.VMEM((SLOTS, QT, DIM), bf16),
            rows, rows, rows, rows, rows, rows,
            pltpu.VMEM((SLOTS, 128), f32),
            pltpu.VMEM((WIDTH, 128, 128), f32),
            pltpu.VMEM((NTILES, TILE * QT, PT), bf16),
            pltpu.VMEM((NTILES * TILE, QT, DIM), f32),
            pltpu.VMEM((NTILES, TILE * QT, DIM), f32),
            pltpu.VMEM((SLOTS, QT, DIM), bf16),
            pltpu.VMEM((SLOTS, QT, DIM), bf16),
            pltpu.VMEM((NR, NPASS, SHARE, DIM), bf16),
            pltpu.VMEM((NR - 1, NPASS, SHARE, DIM), bf16),
            pltpu.VMEM((16, 128), i32),
            pltpu.VMEM((40, 128), i32),
            pltpu.VMEM((8, 128), f32),
            pltpu.SMEM((16, 128), i32),
            pltpu.SMEM((40, 128), i32),
            pltpu.SMEM((8, 128), f32),
        ]
        + [dma(())] * 14,
        compiler_params=pltpu.CompilerParams(
            collective_id=0, has_side_effects=True, vmem_limit_bytes=62 * 1024 * 1024
        ),
    )(query_vecs, passage_vecs, meta)
    return (loss.reshape(NQ), grad_query, grad_passage)


def solution(mesh):
    return jax.shard_map(
        per_device,
        mesh=mesh,
        in_specs=(
            P(("pool", "rep"), None, None),
            P("pool", None, None),
            P(("pool", "rep"), None),
            P(("pool", "rep"), None, None),
            P(("pool", "rep"), None),
        ),
        out_specs=(P(("pool", "rep")), P(("pool", "rep"), None, None), P("pool", "rep", None)),
        check_vma=False,
    )
```

```python
import math

import jax
import jax.numpy as jnp
from jax import lax
from jax.experimental import pallas as pl
from jax.experimental.pallas import tpu as pltpu
from jax.sharding import PartitionSpec as P

MESH = pl.DeviceIdType.MESH
f32, bf16, i32 = jnp.float32, jnp.bfloat16, jnp.int32

TEMPER = 0.05
LOSS_SCALE = 16.0
EPSILON = 1e-06

NP = 64
NR = 4
CAP = 2
NQ = 16
QT = 32
DIM = 128
PT = 256
NPASS = 32
GROUPS = 4
WIDTH = 4
SLOTS = NP * CAP
TILE = 8
NTILES = (SLOTS * WIDTH + NPASS * (TILE - 1)) // TILE
SHARE = PT // NR
RS_CHUNK = 8
UNROLL = 23
HIGH = lax.Precision.HIGHEST


def iota(shape, dim):
    return lax.broadcasted_iota(i32, shape, dim)


def hot(cond, dtype=f32):
    return jnp.where(cond, 1.0, 0.0).astype(dtype)


def index(x, bound):
    return jnp.clip(x.astype(i32), 0, bound - 1)


def dot(a, b):
    return jnp.dot(a.astype(bf16), b.astype(bf16), preferred_element_type=f32)


def dot_nt(a, b):
    return lax.dot_general(
        a.astype(bf16), b.astype(bf16), (((1,), (1,)), ((), ())), preferred_element_type=f32
    )


def hdot(a, b):
    return jnp.dot(a, b, preferred_element_type=f32, precision=HIGH)


def hdot_nt(a, b):
    return lax.dot_general(
        a, b, (((1,), (1,)), ((), ())), preferred_element_type=f32, precision=HIGH
    )


def kernel(
    q_ref, p_any, meta_ref,
    loss_ref, gq_ref, gp_ref,
    p_raw, p_low, q_low, q_send, q_recv, meta_send, meta_recv, sc_send, sc_recv, w_send, w_recv,
    rows_ref, rhs_ref, soft_ref, a_ref, qn_ref, ret_send, ret_recv, rs_send, rs_recv,
    tbla_v, tblb_v, wt_v, tbla, tblb, wt,
    sem_p, sem_tbl, q_ss, q_rs, m_ss, m_rs, s_ss, s_rs, w_ss, w_rs, r_ss, r_rs, x_ss, x_rs,
):
    me = lax.axis_index("pool")
    rep = lax.axis_index("rep")

    def wait_bytes(ref, sem):
        pltpu.make_async_copy(ref, ref, sem).wait()

    def to_pool(src, dst, ss, rs, peer):
        return pltpu.make_async_remote_copy(
            src_ref=src, dst_ref=dst, send_sem=ss, recv_sem=rs, device_id=(peer, rep), device_id_type=MESH
        )

    p_copy = pltpu.make_async_copy(p_any, p_raw, sem_p)
    p_copy.start()

    barrier = pltpu.get_barrier_semaphore()

    def greet(d, _):
        pl.semaphore_signal(
            barrier, inc=1, device_id=(lax.rem(me + d, NP), rep), device_id_type=MESH
        )
        return 0

    lax.fori_loop(1, NP, greet, 0)
    for d in range(1, NR):
        pl.semaphore_signal(
            barrier, inc=1, device_id=(me, lax.rem(rep + d, NR)), device_id_type=MESH
        )

    for a in range(NQ):
        x = q_ref[a].astype(f32)
        inv = lax.rsqrt(jnp.sum(x * x, axis=-1, keepdims=True) + EPSILON)
        q_low[a] = (x * inv).astype(bf16)

    npair = GROUPS * NQ
    mf = meta_ref[...].astype(f32)
    cols = mf.shape[1]
    lane_m = iota((NQ, cols), 1)
    own_col = jnp.concatenate(
        [
            jnp.sum(jnp.where(lane_m == g, mf, 0.0), axis=1, keepdims=True)
            for g in range(GROUPS)
        ],
        axis=0,
    )
    src_r, dst_c = iota((cols, 128), 0), iota((cols, 128), 1)
    loc_w = jnp.concatenate(
        [
            dot(mf, hot((src_r == GROUPS + WIDTH * g + dst_c) & (dst_c < WIDTH)))
            for g in range(GROUPS)
        ],
        axis=0,
    )
    mask_w = [
        dot(mf, hot((src_r == GROUPS + GROUPS * WIDTH + WIDTH * g + dst_c) & (dst_c < WIDTH)))
        for g in range(GROUPS)
    ]
    ra, ca = iota((npair, npair), 0), iota((npair, npair), 1)
    own_row = jnp.sum(jnp.where(ra == ca, own_col, 0.0), axis=0, keepdims=True)
    same = own_col == own_row
    rank_col = jnp.sum(hot(same & (ca % NQ < ra % NQ)), axis=1, keepdims=True)
    rank_row = jnp.sum(hot(same & (ra % NQ < ca % NQ)), axis=0, keepdims=True)
    slot_col = CAP * own_col + rank_col
    slot_row = CAP * own_row + rank_row
    st = hot(slot_col == iota((npair, SLOTS), 1).astype(f32))
    s_hot = hot(slot_row == iota((SLOTS, npair), 0).astype(f32))
    qidx_row = jnp.sum(
        st * (iota((npair, SLOTS), 0) % NQ).astype(f32), axis=0, keepdims=True
    )
    slot_wide = jnp.sum(
        jnp.where(iota((npair, 128), 0) == iota((npair, 128), 1), slot_col, 0.0),
        axis=0, keepdims=True,
    )
    tbla_v[0:8, :] = index(jnp.broadcast_to(qidx_row, (8, 128)), NQ)
    tbla_v[8:16, :] = index(jnp.broadcast_to(slot_wide, (8, 128)), SLOTS)
    tbla_copy = pltpu.make_async_copy(tbla_v, tbla, sem_tbl)
    tbla_copy.start()
    loc_slots = dot(s_hot, loc_w)
    for peer in range(NP):
        meta_send[peer] = loc_slots[CAP * peer : CAP * (peer + 1), :]
    tbla_copy.wait()
    pl.semaphore_wait(barrier, NP - 1 + NR - 1)

    def send_meta(d, _):
        peer = lax.rem(me + d, NP)
        to_pool(meta_send.at[peer], meta_recv.at[me], m_ss, m_rs, peer).start()
        return 0

    lax.fori_loop(1, NP, send_meta, 0)
    meta_recv[me] = meta_send[me]

    def send_q(d, _):
        peer = lax.rem(me + d, NP)
        for k in range(CAP):
            q_send[CAP * peer + k] = q_low[tbla[0, CAP * peer + k]]
        to_pool(
            q_send.at[pl.ds(CAP * peer, CAP)], q_recv.at[pl.ds(CAP * me, CAP)], q_ss, q_rs, peer
        ).start()
        return 0

    lax.fori_loop(1, NP, send_q, 0)
    for k in range(CAP):
        q_recv[CAP * me + k] = q_low[tbla[0, CAP * me + k]]

    p_copy.wait()

    def norm_passage(p, _):
        x = p_raw[p].astype(f32)
        inv = lax.rsqrt(jnp.sum(x * x, axis=-1, keepdims=True) + EPSILON)
        p_low[p] = (x * inv).astype(bf16)
        return 0

    lax.fori_loop(0, NPASS, norm_passage, 0, unroll=2)

    wait_bytes(meta_recv.at[pl.ds(0, NP - 1)], m_rs)
    for peer in range(NP):
        rows_ref[CAP * peer : CAP * (peer + 1), :] = meta_recv[peer]
    loc_r = rows_ref[...]
    r_i, c_i = iota((128, 128), 0), iota((128, 128), 1)
    pc, jc, pr, jr = c_i % NPASS, c_i // NPASS, r_i % NPASS, r_i // NPASS
    one_hot = hot(dot(loc_r, hot((r_i == jc) & (r_i < WIDTH))) == pc.astype(f32))
    before = dot(hot(c_i < r_i), one_hot)
    total = jnp.broadcast_to(jnp.sum(one_hot, axis=0, keepdims=True), (8, 128))
    base = dot(total, hot((pr == pc) & (jr < jc)))[0:1, :]
    tiles = jnp.floor((dot(total, hot(pr == pc)) + (TILE - 1)) * (1.0 / TILE))
    offset = dot(tiles, hot((jr == 0) & (pr < pc)))
    rank = base + before
    rank_tile = jnp.floor(rank * (1.0 / TILE))
    x_tile = one_hot * (offset[0:1, :] + rank_tile)
    x_rest = one_hot * (rank - TILE * rank_tile)
    fold = hot((c_i == jr) & (c_i < WIDTH))
    tile_c = dot(x_tile, fold)
    rest_c = dot(x_rest, fold)
    fold_row = hot(iota((8, 128), 0) == iota((8, 128), 1) // NPASS)
    tile_r = dot_nt(fold_row, x_tile)
    rest_r = dot_nt(fold_row, x_rest)
    loc_rows = dot_nt(hot(iota((8, 128), 0) == iota((8, 128), 1)), loc_r)
    sub8 = iota((8, 128), 0).astype(f32)
    slot_ids = iota((8, 128), 1).astype(f32)
    table = jnp.zeros((16, 128), f32)
    for j in range(WIDTH):
        rest_j = rest_r[j : j + 1, :]
        lhs = jnp.concatenate(
            [
                jnp.where(rest_j == sub8, slot_ids, 0.0),
                jnp.where(rest_j == 0.0, loc_rows[j : j + 1, :], jnp.zeros((8, 128), f32)),
            ],
            axis=0,
        )
        rhs = hot(tile_c[:, j : j + 1] == c_i.astype(f32))
        rhs_ref[j] = rhs
        table = table + dot(lhs, rhs)
    tblb_v[0:8, :] = index(table[0:8], SLOTS)
    tblb_v[8:16, :] = index(table[8:16], NPASS)
    tblb_v[16:24, :] = index(TILE * tile_r + rest_r, NTILES * TILE)
    tblb_v[24:32, :] = index(offset + tiles - 1.0, NTILES)
    tblb_v[32:40, :] = index(tiles, 2)
    tblb_copy = pltpu.make_async_copy(tblb_v, tblb, sem_tbl)
    tblb_copy.start()
    tblb_copy.wait()

    wait_bytes(q_recv.at[pl.ds(0, CAP * (NP - 1))], q_rs)
    ones = jnp.ones((PT, DIM), bf16)
    lane8 = iota((8, 128), 1)

    def forward_tile(t, scores):
        p_tile = p_low[tblb[8, t]]
        q_tile = jnp.concatenate([q_recv[tblb[r, t]] for r in range(TILE)], axis=0)
        sims = lax.dot_general(
            q_tile, p_tile, (((1,), (1,)), ((), ())), preferred_element_type=f32
        )
        soft = jnp.exp2(sims * (math.log2(math.e) / TEMPER)).astype(bf16)
        soft_ref[t] = soft
        both = jnp.dot(
            soft, jnp.concatenate([p_tile, ones], axis=1), preferred_element_type=f32
        )
        sums = both[:, DIM:]
        inv = 1.0 / sums
        a_ref[pl.ds(TILE * t, TILE)] = (both[:, :DIM] * inv).reshape(TILE, QT, DIM)
        qn_ref[t] = q_tile.astype(f32) * inv
        means = (sums * (1.0 / PT)).reshape(TILE, QT // 8, 8, DIM)
        product = means[:, 0]
        for i in range(1, QT // 8):
            product = product * means[:, i]
        logs = jnp.sum(jnp.log(product), axis=1)
        score = TEMPER * (logs + QT * math.log(PT))
        return jnp.where(lane8 == t, score, scores)

    scores = lax.fori_loop(0, NTILES, forward_tile, jnp.zeros((8, 128), f32), unroll=UNROLL)

    sc = jnp.zeros((SLOTS, 128), f32)
    lane_s = iota((SLOTS, 128), 1)
    lane_r = iota((SLOTS, 8), 1).astype(f32)
    for j in range(WIDTH):
        picked = hdot_nt(rhs_ref[j], scores)
        col = jnp.sum(
            jnp.where(rest_c[:, j : j + 1] == lane_r, picked, 0.0), axis=1, keepdims=True
        )
        sc = jnp.where(lane_s == j, col, sc)
    for peer in range(NP):
        sc_send[peer] = sc[CAP * peer : CAP * (peer + 1), :]

    def send_sc(d, _):
        peer = lax.rem(me + d, NP)
        to_pool(sc_send.at[peer], sc_recv.at[me], s_ss, s_rs, peer).start()
        return 0

    lax.fori_loop(1, NP, send_sc, 0)
    sc_recv[me] = sc_send[me]
    wait_bytes(sc_recv.at[pl.ds(0, NP - 1)], s_rs)
    for peer in range(NP):
        rows_ref[CAP * peer : CAP * (peer + 1), :] = sc_recv[peer]

    own_scores = hdot(st, rows_ref[...])
    lane_q = iota((NQ, 128), 1)
    denom = jnp.zeros((NQ, 1), f32)
    exps = []
    for g in range(GROUPS):
        valid = mask_w[g]
        if g == 0:
            valid = jnp.where(lane_q == 0, 1.0, valid)
        e = jnp.exp(own_scores[NQ * g : NQ * (g + 1), :]) * valid
        exps.append(e)
        denom = denom + jnp.sum(e, axis=1, keepdims=True)
    losses = jnp.log(denom) - own_scores[0:NQ, 0:1]
    loss_ref[...] = jnp.sum(
        jnp.where(iota((NQ, NQ), 0) == iota((NQ, NQ), 1), losses, 0.0), axis=0, keepdims=True
    )
    dscore = [LOSS_SCALE * (e / denom) for e in exps]
    dscore[0] = dscore[0] - jnp.where(lane_q == 0, LOSS_SCALE, 0.0)
    w_slots = hdot(s_hot, jnp.concatenate(dscore, axis=0))
    for peer in range(NP):
        w_send[peer] = w_slots[CAP * peer : CAP * (peer + 1), :]

    def send_w(d, _):
        peer = lax.rem(me + d, NP)
        to_pool(w_send.at[peer], w_recv.at[me], w_ss, w_rs, peer).start()
        return 0

    lax.fori_loop(1, NP, send_w, 0)
    w_recv[me] = w_send[me]
    wait_bytes(w_recv.at[pl.ds(0, NP - 1)], w_rs)
    for peer in range(NP):
        rows_ref[CAP * peer : CAP * (peer + 1), :] = w_recv[peer]

    w_rows = hdot_nt(hot(iota((8, 128), 0) == iota((8, 128), 1)), rows_ref[...])
    w_tile = jnp.zeros((8, 128), f32)
    for j in range(WIDTH):
        lhs = jnp.where(rest_r[j : j + 1, :] == sub8, w_rows[j : j + 1, :], 0.0)
        w_tile = w_tile + hdot(lhs, rhs_ref[j])
    wt_v[...] = w_tile
    wt_copy = pltpu.make_async_copy(wt_v, wt, sem_tbl)
    wt_copy.start()
    wt_copy.wait()

    def group_grad(s):
        acc = jnp.zeros((QT, DIM), f32)
        for j in range(WIDTH):
            pos = tblb[16 + j, s]
            acc = acc + wt[pos & (TILE - 1), pos >> 3] * a_ref[pos]
        return acc.astype(bf16)

    def send_ret(d, _):
        peer = lax.rem(me + d, NP)
        for k in range(CAP):
            ret_send[CAP * peer + k] = group_grad(CAP * peer + k)
        to_pool(
            ret_send.at[pl.ds(CAP * peer, CAP)], ret_recv.at[pl.ds(CAP * me, CAP)], r_ss, r_rs, peer
        ).start()
        return 0

    lax.fori_loop(1, NP, send_ret, 0)
    for k in range(CAP):
        ret_recv[CAP * me + k] = group_grad(CAP * me + k)

    def passage_tile(t, acc):
        qs = jnp.concatenate(
            [
                (qn_ref[t, QT * r : QT * (r + 1), :] * wt[r, t]).astype(bf16)
                for r in range(TILE)
            ],
            axis=0,
        )
        grad = lax.dot_general(
            qs, soft_ref[t], (((0,), (0,)), ((), ())), preferred_element_type=f32
        )
        halves = jnp.concatenate([grad[:, :128], grad[:, 128:]], axis=0)
        prev = jnp.maximum(t - 1, 0)
        again = (t > 0) & (tblb[8, t] == tblb[8, prev])
        keep = jnp.where(again, 1.0, 0.0).astype(f32)
        acc = halves + keep * acc
        a_ref[pl.ds(TILE * t, TILE)] = acc.reshape(TILE, QT, DIM)
        return acc

    lax.fori_loop(0, NTILES, passage_tile, jnp.zeros((PT, DIM), f32), unroll=UNROLL)

    for chunk in range(NPASS // RS_CHUNK):

        def cut_passage(i, _):
            p = chunk * RS_CHUNK + i
            last = TILE * tblb[24, p]
            used = tblb[32, p].astype(f32)
            for half in range(2):
                x = jnp.concatenate(
                    [a_ref[last + 4 * half + m] for m in range(4)], axis=0
                )
                y = (x * used).T.astype(bf16)
                for part in range(2):
                    rs_send[2 * half + part, p] = y[SHARE * part : SHARE * (part + 1), :]
            return 0

        lax.fori_loop(0, RS_CHUNK, cut_passage, 0, unroll=RS_CHUNK)
        rows = pl.ds(chunk * RS_CHUNK, RS_CHUNK)
        for d in range(1, NR):
            target = lax.rem(rep + d, NR)
            pltpu.make_async_remote_copy(
                src_ref=rs_send.at[target, rows],
                dst_ref=rs_recv.at[d - 1, rows],
                send_sem=x_ss,
                recv_sem=x_rs,
                device_id=(me, target),
                device_id_type=MESH,
            ).start()

    wait_bytes(ret_recv.at[pl.ds(0, CAP * (NP - 1))], r_rs)

    def finish_query(a, _):
        x = q_ref[a].astype(f32)
        inv = lax.rsqrt(jnp.sum(x * x, axis=-1, keepdims=True) + EPSILON)
        unit = x * inv
        up = jnp.zeros((QT, DIM), f32)
        for g in range(GROUPS):
            up = up + ret_recv[tbla[8, NQ * g + a]].astype(f32)
        gq_ref[a] = inv * (up - unit * jnp.sum(unit * up, axis=-1, keepdims=True))
        return 0

    lax.fori_loop(0, NQ, finish_query, 0, unroll=4)

    wait_bytes(rs_recv, x_rs)
    start = pl.multiple_of(rep * SHARE, SHARE)

    def finish_passage(p, _):
        x = p_raw[p, pl.ds(start, SHARE), :].astype(f32)
        inv = lax.rsqrt(jnp.sum(x * x, axis=-1, keepdims=True) + EPSILON)
        unit = x * inv
        up = rs_send[rep, p].astype(f32)
        for d in range(NR - 1):
            up = up + rs_recv[d, p].astype(f32)
        gp_ref[p] = inv * (up - unit * jnp.sum(unit * up, axis=-1, keepdims=True))
        return 0

    lax.fori_loop(0, NPASS, finish_passage, 0, unroll=4)

    wait_bytes(meta_send.at[pl.ds(0, NP - 1)], m_ss)
    wait_bytes(q_send.at[pl.ds(0, CAP * (NP - 1))], q_ss)
    wait_bytes(sc_send.at[pl.ds(0, NP - 1)], s_ss)
    wait_bytes(w_send.at[pl.ds(0, NP - 1)], w_ss)
    wait_bytes(ret_send.at[pl.ds(0, CAP * (NP - 1))], r_ss)
    wait_bytes(rs_recv, x_ss)


def per_device(query_vecs, passage_vecs, owner_ids, local_ids, cand_mask):
    meta = jnp.concatenate(
        [owner_ids, local_ids.reshape(NQ, GROUPS * WIDTH), cand_mask], axis=1
    )
    vmem = pl.BlockSpec(memory_space=pltpu.VMEM)
    rows = pltpu.VMEM((NP, CAP, 128), f32)
    dma = pltpu.SemaphoreType.DMA
    loss, grad_query, grad_passage = pl.pallas_call(
        kernel,
        out_shape=(
            jax.ShapeDtypeStruct((1, NQ), f32),
            jax.ShapeDtypeStruct((NQ, QT, DIM), f32),
            jax.ShapeDtypeStruct((NPASS, SHARE, DIM), f32),
        ),
        in_specs=[vmem, pl.BlockSpec(memory_space=pl.ANY), vmem],
        out_specs=[vmem, vmem, vmem],
        scratch_shapes=[
            pltpu.VMEM((NPASS, PT, DIM), bf16),
            pltpu.VMEM((NPASS, PT, DIM), bf16),
            pltpu.VMEM((NQ, QT, DIM), bf16),
            pltpu.VMEM((SLOTS, QT, DIM), bf16),
            pltpu.VMEM((SLOTS, QT, DIM), bf16),
            rows, rows, rows, rows, rows, rows,
            pltpu.VMEM((SLOTS, 128), f32),
            pltpu.VMEM((WIDTH, 128, 128), f32),
            pltpu.VMEM((NTILES, TILE * QT, PT), bf16),
            pltpu.VMEM((NTILES * TILE, QT, DIM), f32),
            pltpu.VMEM((NTILES, TILE * QT, DIM), f32),
            pltpu.VMEM((SLOTS, QT, DIM), bf16),
            pltpu.VMEM((SLOTS, QT, DIM), bf16),
            pltpu.VMEM((NR, NPASS, SHARE, DIM), bf16),
            pltpu.VMEM((NR - 1, NPASS, SHARE, DIM), bf16),
            pltpu.VMEM((16, 128), i32),
            pltpu.VMEM((40, 128), i32),
            pltpu.VMEM((8, 128), f32),
            pltpu.SMEM((16, 128), i32),
            pltpu.SMEM((40, 128), i32),
            pltpu.SMEM((8, 128), f32),
        ]
        + [dma(())] * 14,
        compiler_params=pltpu.CompilerParams(
            collective_id=0, has_side_effects=True, vmem_limit_bytes=62 * 1024 * 1024
        ),
    )(query_vecs, passage_vecs, meta)
    return (loss.reshape(NQ), grad_query, grad_passage)


def solution(mesh):
    return jax.shard_map(
        per_device,
        mesh=mesh,
        in_specs=(
            P(("pool", "rep"), None, None),
            P("pool", None, None),
            P(("pool", "rep"), None),
            P(("pool", "rep"), None, None),
            P(("pool", "rep"), None),
        ),
        out_specs=(P(("pool", "rep")), P(("pool", "rep"), None, None), P("pool", "rep", None)),
        check_vma=False,
    )
```

```python
import math

import jax
import jax.numpy as jnp
from jax import lax
from jax.experimental import pallas as pl
from jax.experimental.pallas import tpu as pltpu
from jax.sharding import PartitionSpec as P

MESH = pl.DeviceIdType.MESH
f32, bf16, i32 = jnp.float32, jnp.bfloat16, jnp.int32

TEMPER = 0.05
LOSS_SCALE = 16.0
EPSILON = 1e-06

NP = 64
NR = 4
NZ = 8
NC = NP // NZ
CAP = 2
NQ = 16
QT = 32
DIM = 128
PT = 256
NPASS = 32
GROUPS = 4
WIDTH = 4
SLOTS = NP * CAP
TILE = 8
NTILES = (SLOTS * WIDTH + NPASS * (TILE - 1)) // TILE
SHARE = PT // NR
RS_CHUNK = 8
UNROLL = 23
HIGH = lax.Precision.HIGHEST


def iota(shape, dim):
    return lax.broadcasted_iota(i32, shape, dim)


def hot(cond, dtype=f32):
    return jnp.where(cond, 1.0, 0.0).astype(dtype)


def index(x, bound):
    return jnp.clip(x.astype(i32), 0, bound - 1)


def dot(a, b):
    return jnp.dot(a.astype(bf16), b.astype(bf16), preferred_element_type=f32)


def dot_nt(a, b):
    return lax.dot_general(
        a.astype(bf16), b.astype(bf16), (((1,), (1,)), ((), ())), preferred_element_type=f32
    )


def hdot(a, b):
    return jnp.dot(a, b, preferred_element_type=f32, precision=HIGH)


def hdot_nt(a, b):
    return lax.dot_general(
        a, b, (((1,), (1,)), ((), ())), preferred_element_type=f32, precision=HIGH
    )


def kernel(
    q_ref, p_any, own_ref, loc_ref, mask_ref,
    loss_ref, gq_ref, gp_ref,
    p_raw, p_low, q_low, plus1, plus2, plus3, minus1, minus2, minus3, far, q_send, q_recv,
    m_a, m_b, m_c, s_a, s_b, s_c, w_a, w_b, w_c,
    rows_ref, rhs_ref, soft_ref, a_ref, qn_ref, ret_send, ret_recv, rs_send, rs_recv,
    tbla_v, tblm_v, tblb_v, wt_v, tbla, tblm, tblb, wt,
    sem_p, sem_tbl, hop_s, plus_r, minus_r, q_ss, q_rs, m_sem, s_sem, w_sem, r_ss, r_rs, x_ss, x_rs,
):
    me = lax.axis_index("pool")
    rep = lax.axis_index("rep")
    z = lax.div(me, NC)
    c = lax.rem(me, NC)

    def wait_bytes(ref, sem):
        pltpu.make_async_copy(ref, ref, sem).wait()

    def to_pool(src, dst, ss, rs, peer):
        return pltpu.make_async_remote_copy(
            src_ref=src, dst_ref=dst, send_sem=ss, recv_sem=rs, device_id=(peer, rep), device_id_type=MESH
        )

    def along_z(e):
        return NC * lax.rem(z + NZ + e, NZ) + c

    def in_plane(e):
        return NC * z + lax.rem(c + e, NC)

    def first_hop(send, mid, sems):
        for e in range(1, NZ):
            target = lax.rem(z + e, NZ)
            to_pool(send.at[target], mid.at[z], sems.at[0], sems.at[1], NC * target + c).start()
        mid[z] = send[z]

    def second_hop(mid, recv, sems):
        wait_bytes(mid.at[pl.ds(0, NZ - 1)], sems.at[1])
        for e in range(1, NC):
            target = lax.rem(c + e, NC)
            to_pool(mid.at[:, target], recv.at[:, c], sems.at[2], sems.at[3], NC * z + target).start()
        for k in range(NZ):
            recv[k, c] = mid[k, c]

    def arrived(recv, sems):
        wait_bytes(recv.at[pl.ds(0, NC - 1)], sems.at[3])

    def put_rows(send, rows):
        for peer in range(NP):
            send[peer // NC, peer % NC] = rows[CAP * peer : CAP * (peer + 1), :]

    def take_rows(recv):
        for peer in range(NP):
            rows_ref[CAP * peer : CAP * (peer + 1), :] = recv[peer // NC, peer % NC]

    p_copy = pltpu.make_async_copy(p_any, p_raw, sem_p)
    p_copy.start()

    barrier = pltpu.get_barrier_semaphore()
    for e in range(1, NZ):
        pl.semaphore_signal(barrier, inc=1, device_id=(along_z(e), rep), device_id_type=MESH)
    for e in range(1, NC):
        pl.semaphore_signal(barrier, inc=1, device_id=(in_plane(e), rep), device_id_type=MESH)
    for d in range(1, NR):
        pl.semaphore_signal(
            barrier, inc=1, device_id=(me, lax.rem(rep + d, NR)), device_id_type=MESH
        )

    for a in range(NQ):
        x = q_ref[a].astype(f32)
        inv = lax.rsqrt(jnp.sum(x * x, axis=-1, keepdims=True) + EPSILON)
        q_low[a] = (x * inv).astype(bf16)

    npair = GROUPS * NQ
    eye = iota((NQ, NQ), 0) == iota((NQ, NQ), 1)
    own_f = own_ref[...].astype(f32)
    own_col = jnp.concatenate(
        [
            jnp.sum(jnp.where(eye, own_f[g : g + 1, :], 0.0), axis=1, keepdims=True)
            for g in range(GROUPS)
        ],
        axis=0,
    )
    loc_f = dot_nt(hot(eye), loc_ref[...].astype(f32))
    mask_f = mask_ref[...].astype(f32)
    src_r, dst_c = iota((NQ, 128), 0), iota((NQ, 128), 1)
    places = [hot((src_r == WIDTH * g + dst_c) & (dst_c < WIDTH)) for g in range(GROUPS)]
    loc_w = jnp.concatenate([dot(loc_f, place) for place in places], axis=0)
    mask_w = [dot(mask_f, place) for place in places]
    pair_q = (iota((npair, 128), 0) % NQ).astype(f32)
    loc_w = jnp.where(iota((npair, 128), 1) == WIDTH, pair_q, loc_w)
    ra, ca = iota((npair, npair), 0), iota((npair, npair), 1)
    own_row = jnp.sum(jnp.where(ra == ca, own_col, 0.0), axis=0, keepdims=True)
    same = own_col == own_row
    rank_col = jnp.sum(hot(same & (ca % NQ < ra % NQ)), axis=1, keepdims=True)
    rank_row = jnp.sum(hot(same & (ra % NQ < ca % NQ)), axis=0, keepdims=True)
    slot_col = CAP * own_col + rank_col
    slot_row = CAP * own_row + rank_row
    st = hot(slot_col == iota((npair, SLOTS), 1).astype(f32))
    s_hot = hot(slot_row == iota((SLOTS, npair), 0).astype(f32))
    slot_wide = jnp.sum(
        jnp.where(iota((npair, 128), 0) == iota((npair, 128), 1), slot_col, 0.0),
        axis=0, keepdims=True,
    )
    tbla_v[...] = index(jnp.broadcast_to(slot_wide, (8, 128)), SLOTS)
    tbla_copy = pltpu.make_async_copy(tbla_v, tbla, sem_tbl)
    tbla_copy.start()
    put_rows(m_a, dot(s_hot, loc_w))
    tbla_copy.wait()
    pl.semaphore_wait(barrier, NZ - 1 + NC - 1 + NR - 1)

    first_hop(m_a, m_b, m_sem)

    plus, minus = [q_low, plus1, plus2, plus3], [q_low, minus1, minus2, minus3]
    half = NQ // 2

    def pass_on(h):
        if h < NZ // 2 - 1:
            to_pool(plus[h], plus[h + 1], hop_s, plus_r.at[h], along_z(1)).start()
            to_pool(minus[h], minus[h + 1], hop_s, minus_r.at[h], along_z(-1)).start()
        else:
            low, top = pl.ds(0, half), pl.ds(half, half)
            to_pool(plus[h].at[low], far.at[low], hop_s, plus_r.at[h], along_z(1)).start()
            to_pool(minus[h].at[top], far.at[top], hop_s, minus_r.at[h], along_z(-1)).start()

    pass_on(0)

    second_hop(m_b, m_c, m_sem)
    take_rows(m_b)
    r_i, c_i = iota((128, 128), 0), iota((128, 128), 1)
    picked = jnp.sum(
        jnp.where(r_i == c_i, rows_ref[:, WIDTH : WIDTH + 1], 0.0), axis=0, keepdims=True
    )
    tblm_v[...] = index(jnp.broadcast_to(picked, (8, 128)), NQ)
    tblm_copy = pltpu.make_async_copy(tblm_v, tblm, sem_tbl)
    tblm_copy.start()
    tblm_copy.wait()

    def deliver(block, source):
        for e in range(1, NC):
            target = lax.rem(c + e, NC)
            row = CAP * (NC * source + target)
            for k in range(CAP):
                q_send[row + k] = block[tblm[0, row + k]]
            to_pool(
                q_send.at[pl.ds(row, CAP)],
                q_recv.at[pl.ds(CAP * (NC * source + c), CAP)],
                q_ss, q_rs, NC * z + target,
            ).start()
        row = CAP * (NC * source + c)
        for k in range(CAP):
            q_recv[row + k] = block[tblm[0, row + k]]

    def norm_passage(p, _):
        x = p_raw[p].astype(f32)
        inv = lax.rsqrt(jnp.sum(x * x, axis=-1, keepdims=True) + EPSILON)
        p_low[p] = (x * inv).astype(bf16)
        return 0

    deliver(q_low, z)
    p_copy.wait()
    for h in range(1, NZ // 2):
        wait_bytes(plus[h], plus_r.at[h - 1])
        wait_bytes(minus[h], minus_r.at[h - 1])
        pass_on(h)
        deliver(plus[h], lax.rem(z + NZ - h, NZ))
        deliver(minus[h], lax.rem(z + h, NZ))
        part = NPASS // (NZ // 2)
        lax.fori_loop(part * (h - 1), part * h, norm_passage, 0, unroll=2)
    lax.fori_loop(NPASS - part, NPASS, norm_passage, 0, unroll=2)

    arrived(m_c, m_sem)
    take_rows(m_c)
    loc_r = rows_ref[...]
    pc, jc, pr, jr = c_i % NPASS, c_i // NPASS, r_i % NPASS, r_i // NPASS
    one_hot = hot(dot(loc_r, hot((r_i == jc) & (r_i < WIDTH))) == pc.astype(f32))
    before = dot(hot(c_i < r_i), one_hot)
    total = jnp.broadcast_to(jnp.sum(one_hot, axis=0, keepdims=True), (8, 128))
    base = dot(total, hot((pr == pc) & (jr < jc)))[0:1, :]
    tiles = jnp.floor((dot(total, hot(pr == pc)) + (TILE - 1)) * (1.0 / TILE))
    offset = dot(tiles, hot((jr == 0) & (pr < pc)))
    rank = base + before
    rank_tile = jnp.floor(rank * (1.0 / TILE))
    x_tile = one_hot * (offset[0:1, :] + rank_tile)
    x_rest = one_hot * (rank - TILE * rank_tile)
    fold = hot((c_i == jr) & (c_i < WIDTH))
    tile_c = dot(x_tile, fold)
    rest_c = dot(x_rest, fold)
    fold_row = hot(iota((8, 128), 0) == iota((8, 128), 1) // NPASS)
    tile_r = dot_nt(fold_row, x_tile)
    rest_r = dot_nt(fold_row, x_rest)
    loc_rows = dot_nt(hot(iota((8, 128), 0) == iota((8, 128), 1)), loc_r)
    sub8 = iota((8, 128), 0).astype(f32)
    slot_ids = iota((8, 128), 1).astype(f32)
    table = jnp.zeros((16, 128), f32)
    for j in range(WIDTH):
        rest_j = rest_r[j : j + 1, :]
        lhs = jnp.concatenate(
            [
                jnp.where(rest_j == sub8, slot_ids, 0.0),
                jnp.where(rest_j == 0.0, loc_rows[j : j + 1, :], jnp.zeros((8, 128), f32)),
            ],
            axis=0,
        )
        rhs = hot(tile_c[:, j : j + 1] == c_i.astype(f32))
        rhs_ref[j] = rhs
        table = table + dot(lhs, rhs)
    tblb_v[0:8, :] = index(table[0:8], SLOTS)
    tblb_v[8:16, :] = index(table[8:16], NPASS)
    tblb_v[16:24, :] = index(TILE * tile_r + rest_r, NTILES * TILE)
    tblb_v[24:32, :] = index(offset + tiles - 1.0, NTILES)
    tblb_v[32:40, :] = index(tiles, 2)
    tblb_copy = pltpu.make_async_copy(tblb_v, tblb, sem_tbl)
    tblb_copy.start()
    tblb_copy.wait()

    wait_bytes(far.at[pl.ds(0, half)], plus_r.at[NZ // 2 - 1])
    wait_bytes(far.at[pl.ds(half, half)], minus_r.at[NZ // 2 - 1])
    deliver(far, lax.rem(z + NZ // 2, NZ))
    wait_bytes(q_recv.at[pl.ds(0, CAP * NZ * (NC - 1))], q_rs)
    ones = jnp.ones((PT, DIM), bf16)
    lane8 = iota((8, 128), 1)

    def forward_tile(t, scores):
        p_tile = p_low[tblb[8, t]]
        q_tile = jnp.concatenate([q_recv[tblb[r, t]] for r in range(TILE)], axis=0)
        sims = lax.dot_general(
            q_tile, p_tile, (((1,), (1,)), ((), ())), preferred_element_type=f32
        )
        soft = jnp.exp2(sims * (math.log2(math.e) / TEMPER)).astype(bf16)
        soft_ref[t] = soft
        both = jnp.dot(
            soft, jnp.concatenate([p_tile, ones], axis=1), preferred_element_type=f32
        )
        sums = both[:, DIM:]
        inv = 1.0 / sums
        a_ref[pl.ds(TILE * t, TILE)] = (both[:, :DIM] * inv).reshape(TILE, QT, DIM)
        qn_ref[t] = q_tile.astype(f32) * inv
        means = (sums * (1.0 / PT)).reshape(TILE, QT // 8, 8, DIM)
        product = means[:, 0]
        for i in range(1, QT // 8):
            product = product * means[:, i]
        logs = jnp.sum(jnp.log(product), axis=1)
        score = TEMPER * (logs + QT * math.log(PT))
        return jnp.where(lane8 == t, score, scores)

    scores = lax.fori_loop(0, NTILES, forward_tile, jnp.zeros((8, 128), f32), unroll=UNROLL)

    sc = jnp.zeros((SLOTS, 128), f32)
    lane_s = iota((SLOTS, 128), 1)
    lane_r = iota((SLOTS, 8), 1).astype(f32)
    for j in range(WIDTH):
        picked = hdot_nt(rhs_ref[j], scores)
        col = jnp.sum(
            jnp.where(rest_c[:, j : j + 1] == lane_r, picked, 0.0), axis=1, keepdims=True
        )
        sc = jnp.where(lane_s == j, col, sc)
    put_rows(s_a, sc)
    first_hop(s_a, s_b, s_sem)
    second_hop(s_b, s_c, s_sem)
    arrived(s_c, s_sem)
    take_rows(s_c)

    own_scores = hdot(st, rows_ref[...])
    lane_q = iota((NQ, 128), 1)
    denom = jnp.zeros((NQ, 1), f32)
    exps = []
    for g in range(GROUPS):
        valid = mask_w[g]
        if g == 0:
            valid = jnp.where(lane_q == 0, 1.0, valid)
        e = jnp.exp(own_scores[NQ * g : NQ * (g + 1), :]) * valid
        exps.append(e)
        denom = denom + jnp.sum(e, axis=1, keepdims=True)
    losses = jnp.log(denom) - own_scores[0:NQ, 0:1]
    loss_ref[...] = jnp.sum(
        jnp.where(iota((NQ, NQ), 0) == iota((NQ, NQ), 1), losses, 0.0), axis=0, keepdims=True
    )
    dscore = [LOSS_SCALE * (e / denom) for e in exps]
    dscore[0] = dscore[0] - jnp.where(lane_q == 0, LOSS_SCALE, 0.0)
    w_slots = hdot(s_hot, jnp.concatenate(dscore, axis=0))
    put_rows(w_a, w_slots)
    first_hop(w_a, w_b, w_sem)
    second_hop(w_b, w_c, w_sem)
    arrived(w_c, w_sem)
    take_rows(w_c)

    w_rows = hdot_nt(hot(iota((8, 128), 0) == iota((8, 128), 1)), rows_ref[...])
    w_tile = jnp.zeros((8, 128), f32)
    for j in range(WIDTH):
        lhs = jnp.where(rest_r[j : j + 1, :] == sub8, w_rows[j : j + 1, :], 0.0)
        w_tile = w_tile + hdot(lhs, rhs_ref[j])
    wt_v[...] = w_tile
    wt_copy = pltpu.make_async_copy(wt_v, wt, sem_tbl)
    wt_copy.start()
    wt_copy.wait()

    def group_grad(s):
        acc = jnp.zeros((QT, DIM), f32)
        for j in range(WIDTH):
            pos = tblb[16 + j, s]
            acc = acc + wt[pos & (TILE - 1), pos >> 3] * a_ref[pos]
        return acc.astype(bf16)

    def send_ret(d, _):
        peer = lax.rem(me + d, NP)
        for k in range(CAP):
            ret_send[CAP * peer + k] = group_grad(CAP * peer + k)
        to_pool(
            ret_send.at[pl.ds(CAP * peer, CAP)], ret_recv.at[pl.ds(CAP * me, CAP)], r_ss, r_rs, peer
        ).start()
        return 0

    lax.fori_loop(1, NP, send_ret, 0)
    for k in range(CAP):
        ret_recv[CAP * me + k] = group_grad(CAP * me + k)

    def passage_tile(t, acc):
        qs = jnp.concatenate(
            [
                (qn_ref[t, QT * r : QT * (r + 1), :] * wt[r, t]).astype(bf16)
                for r in range(TILE)
            ],
            axis=0,
        )
        grad = lax.dot_general(
            qs, soft_ref[t], (((0,), (0,)), ((), ())), preferred_element_type=f32
        )
        halves = jnp.concatenate([grad[:, :128], grad[:, 128:]], axis=0)
        prev = jnp.maximum(t - 1, 0)
        again = (t > 0) & (tblb[8, t] == tblb[8, prev])
        keep = jnp.where(again, 1.0, 0.0).astype(f32)
        acc = halves + keep * acc
        a_ref[pl.ds(TILE * t, TILE)] = acc.reshape(TILE, QT, DIM)
        return acc

    lax.fori_loop(0, NTILES, passage_tile, jnp.zeros((PT, DIM), f32), unroll=UNROLL)

    for chunk in range(NPASS // RS_CHUNK):

        def cut_passage(i, _):
            p = chunk * RS_CHUNK + i
            last = TILE * tblb[24, p]
            used = tblb[32, p].astype(f32)
            for half in range(2):
                x = jnp.concatenate(
                    [a_ref[last + 4 * half + m] for m in range(4)], axis=0
                )
                y = (x * used).T.astype(bf16)
                for part in range(2):
                    rs_send[2 * half + part, p] = y[SHARE * part : SHARE * (part + 1), :]
            return 0

        lax.fori_loop(0, RS_CHUNK, cut_passage, 0, unroll=RS_CHUNK)
        rows = pl.ds(chunk * RS_CHUNK, RS_CHUNK)
        for d in range(1, NR):
            target = lax.rem(rep + d, NR)
            pltpu.make_async_remote_copy(
                src_ref=rs_send.at[target, rows],
                dst_ref=rs_recv.at[d - 1, rows],
                send_sem=x_ss,
                recv_sem=x_rs,
                device_id=(me, target),
                device_id_type=MESH,
            ).start()

    wait_bytes(ret_recv.at[pl.ds(0, CAP * (NP - 1))], r_rs)

    def finish_query(a, _):
        x = q_ref[a].astype(f32)
        inv = lax.rsqrt(jnp.sum(x * x, axis=-1, keepdims=True) + EPSILON)
        unit = x * inv
        up = jnp.zeros((QT, DIM), f32)
        for g in range(GROUPS):
            up = up + ret_recv[tbla[0, NQ * g + a]].astype(f32)
        gq_ref[a] = inv * (up - unit * jnp.sum(unit * up, axis=-1, keepdims=True))
        return 0

    lax.fori_loop(0, NQ, finish_query, 0, unroll=4)

    wait_bytes(rs_recv, x_rs)
    start = pl.multiple_of(rep * SHARE, SHARE)

    def finish_passage(p, _):
        x = p_raw[p, pl.ds(start, SHARE), :].astype(f32)
        inv = lax.rsqrt(jnp.sum(x * x, axis=-1, keepdims=True) + EPSILON)
        unit = x * inv
        up = rs_send[rep, p].astype(f32)
        for d in range(NR - 1):
            up = up + rs_recv[d, p].astype(f32)
        gp_ref[p] = inv * (up - unit * jnp.sum(unit * up, axis=-1, keepdims=True))
        return 0

    lax.fori_loop(0, NPASS, finish_passage, 0, unroll=4)

    for send, sems in ((m_a, m_sem), (s_a, s_sem), (w_a, w_sem)):
        wait_bytes(send.at[pl.ds(0, NZ - 1)], sems.at[0])
        wait_bytes(send.at[pl.ds(0, NC - 1)], sems.at[2])
    wait_bytes(q_send.at[pl.ds(0, NQ * (NZ - 1))], hop_s)
    wait_bytes(q_send.at[pl.ds(0, CAP * NZ * (NC - 1))], q_ss)
    wait_bytes(ret_send.at[pl.ds(0, CAP * (NP - 1))], r_ss)
    wait_bytes(rs_recv, x_ss)


def leave(loss_in, gq_in, gp_in, loss_out, gq_out, gp_out, sems):
    copies = [
        pltpu.make_async_copy(src, dst, sems.at[i])
        for i, (src, dst) in enumerate(
            ((gp_in, gp_out), (gq_in, gq_out), (loss_in, loss_out))
        )
    ]
    for copy in copies:
        copy.start()
    for copy in copies:
        copy.wait()


def per_device(query_vecs, passage_vecs, owner_ids, local_ids, cand_mask):
    vmem = pl.BlockSpec(memory_space=pltpu.VMEM)
    anywhere = pl.BlockSpec(memory_space=pl.ANY)
    rows = pltpu.VMEM((NZ, NC, CAP, 128), f32)
    block = pltpu.VMEM((NQ, QT, DIM), bf16)
    dma = pltpu.SemaphoreType.DMA
    outs = (
        jax.ShapeDtypeStruct((1, NQ), f32),
        jax.ShapeDtypeStruct((NQ, QT, DIM), f32),
        jax.ShapeDtypeStruct((NPASS, SHARE, DIM), f32),
    )
    results = pl.pallas_call(
        kernel,
        out_shape=outs,
        in_specs=[vmem, anywhere, vmem, vmem, vmem],
        out_specs=[vmem, vmem, vmem],
        scratch_shapes=[
            pltpu.VMEM((NPASS, PT, DIM), bf16),
            pltpu.VMEM((NPASS, PT, DIM), bf16),
        ]
        + [block] * 8
        + [
            pltpu.VMEM((SLOTS, QT, DIM), bf16),
            pltpu.VMEM((SLOTS, QT, DIM), bf16),
        ]
        + [rows] * 9
        + [
            pltpu.VMEM((SLOTS, 128), f32),
            pltpu.VMEM((WIDTH, 128, 128), f32),
            pltpu.VMEM((NTILES, TILE * QT, PT), bf16),
            pltpu.VMEM((NTILES * TILE, QT, DIM), f32),
            pltpu.VMEM((NTILES, TILE * QT, DIM), f32),
            pltpu.VMEM((SLOTS, QT, DIM), bf16),
            pltpu.VMEM((SLOTS, QT, DIM), bf16),
            pltpu.VMEM((NR, NPASS, SHARE, DIM), bf16),
            pltpu.VMEM((NR - 1, NPASS, SHARE, DIM), bf16),
            pltpu.VMEM((8, 128), i32),
            pltpu.VMEM((8, 128), i32),
            pltpu.VMEM((40, 128), i32),
            pltpu.VMEM((8, 128), f32),
            pltpu.SMEM((8, 128), i32),
            pltpu.SMEM((8, 128), i32),
            pltpu.SMEM((40, 128), i32),
            pltpu.SMEM((8, 128), f32),
        ]
        + [dma(()), dma(()), dma(()), dma((NZ // 2,)), dma((NZ // 2,)), dma(()), dma(())]
        + [dma((4,))] * 3
        + [dma(())] * 4,
        compiler_params=pltpu.CompilerParams(
            collective_id=0, has_side_effects=True, vmem_limit_bytes=62 * 1024 * 1024
        ),
    )(
        query_vecs,
        passage_vecs,
        owner_ids.T,
        local_ids.transpose(1, 2, 0).reshape(GROUPS * WIDTH, NQ),
        cand_mask,
    )
    loss, grad_query, grad_passage = pl.pallas_call(
        leave,
        out_shape=outs,
        in_specs=[anywhere] * 3,
        out_specs=[anywhere] * 3,
        scratch_shapes=[dma((3,))],
    )(*results)
    return (loss.reshape(NQ), grad_query, grad_passage)


def solution(mesh):
    return jax.shard_map(
        per_device,
        mesh=mesh,
        in_specs=(
            P(("pool", "rep"), None, None),
            P("pool", None, None),
            P(("pool", "rep"), None),
            P(("pool", "rep"), None, None),
            P(("pool", "rep"), None),
        ),
        out_specs=(P(("pool", "rep")), P(("pool", "rep"), None, None), P("pool", "rep", None)),
        check_vma=False,
    )
```

```python
import math

import jax
import jax.numpy as jnp
from jax import lax
from jax.experimental import pallas as pl
from jax.experimental.pallas import tpu as pltpu
from jax.sharding import PartitionSpec as P

MESH = pl.DeviceIdType.MESH
f32, bf16, i32 = jnp.float32, jnp.bfloat16, jnp.int32

TEMPER = 0.05
LOSS_SCALE = 16.0
EPSILON = 1e-06

NP = 64
NR = 4
NZ = 8
NC = NP // NZ
PIECES = 4
CAP = 2
NQ = 16
QT = 32
DIM = 128
PT = 256
NPASS = 32
GROUPS = 4
WIDTH = 4
SLOTS = NP * CAP
TILE = 8
NTILES = (SLOTS * WIDTH + NPASS * (TILE - 1)) // TILE
SHARE = PT // NR
RS_CHUNK = 8
UNROLL = 23
HIGH = lax.Precision.HIGHEST


def iota(shape, dim):
    return lax.broadcasted_iota(i32, shape, dim)


def hot(cond, dtype=f32):
    return jnp.where(cond, 1.0, 0.0).astype(dtype)


def index(x, bound):
    return jnp.clip(x.astype(i32), 0, bound - 1)


def dot(a, b):
    return jnp.dot(a.astype(bf16), b.astype(bf16), preferred_element_type=f32)


def dot_nt(a, b):
    return lax.dot_general(
        a.astype(bf16), b.astype(bf16), (((1,), (1,)), ((), ())), preferred_element_type=f32
    )


def hdot(a, b):
    return jnp.dot(a, b, preferred_element_type=f32, precision=HIGH)


def hdot_nt(a, b):
    return lax.dot_general(
        a, b, (((1,), (1,)), ((), ())), preferred_element_type=f32, precision=HIGH
    )


def kernel(
    q_ref, p_any, own_ref, loc_ref, mask_ref,
    loss_ref, uq_ref, up_ref,
    p_raw, p_low, q_low, plus1, plus2, plus3, minus1, minus2, minus3, far, q_send, q_recv,
    m_a, m_b, m_c, s_a, s_b, s_c, w_a, w_b, w_c,
    rows_ref, rhs_ref, soft_ref, a_ref, qn_ref, ret_send, ret_recv, rs_send, rs_recv, via_plus, via_minus, sum_plus, sum_minus,
    tbla_v, tblm_v, tblb_v, wt_v, tbla, tblm, tblb, wt,
    sem_p, sem_tbl, hop_s, plus_r, minus_r, q_ss, q_rs, m_sem, s_sem, w_sem, r_ss, r_rs, x_ss, x_rs, v_rs,
):
    me = lax.axis_index("pool")
    rep = lax.axis_index("rep")
    z = lax.div(me, NC)
    c = lax.rem(me, NC)

    def wait_bytes(ref, sem):
        pltpu.make_async_copy(ref, ref, sem).wait()

    def to_pool(src, dst, ss, rs, peer):
        return pltpu.make_async_remote_copy(
            src_ref=src, dst_ref=dst, send_sem=ss, recv_sem=rs, device_id=(peer, rep), device_id_type=MESH
        )

    def along_z(e):
        return NC * lax.rem(z + NZ + e, NZ) + c

    def in_plane(e):
        return NC * z + lax.rem(c + e, NC)

    def first_hop(send, mid, sems):
        for e in range(1, NZ):
            target = lax.rem(z + e, NZ)
            to_pool(send.at[target], mid.at[z], sems.at[0], sems.at[1], NC * target + c).start()
        mid[z] = send[z]

    def second_hop(mid, recv, sems):
        wait_bytes(mid.at[pl.ds(0, NZ - 1)], sems.at[1])
        for e in range(1, NC):
            target = lax.rem(c + e, NC)
            to_pool(mid.at[:, target], recv.at[:, c], sems.at[2], sems.at[3], NC * z + target).start()
        for k in range(NZ):
            recv[k, c] = mid[k, c]

    def arrived(recv, sems):
        wait_bytes(recv.at[pl.ds(0, NC - 1)], sems.at[3])

    def put_rows(send, rows):
        for peer in range(NP):
            send[peer // NC, peer % NC] = rows[CAP * peer : CAP * (peer + 1), :]

    def take_rows(recv):
        for peer in range(NP):
            rows_ref[CAP * peer : CAP * (peer + 1), :] = recv[peer // NC, peer % NC]

    p_copy = pltpu.make_async_copy(p_any, p_raw, sem_p)
    p_copy.start()

    barrier = pltpu.get_barrier_semaphore()
    for e in range(1, NZ):
        pl.semaphore_signal(barrier, inc=1, device_id=(along_z(e), rep), device_id_type=MESH)
    for e in range(1, NC):
        pl.semaphore_signal(barrier, inc=1, device_id=(in_plane(e), rep), device_id_type=MESH)
    for d in range(1, NR):
        pl.semaphore_signal(
            barrier, inc=1, device_id=(me, lax.rem(rep + d, NR)), device_id_type=MESH
        )

    for a in range(NQ):
        x = q_ref[a].astype(f32)
        inv = lax.rsqrt(jnp.sum(x * x, axis=-1, keepdims=True) + EPSILON)
        q_low[a] = (x * inv).astype(bf16)

    npair = GROUPS * NQ
    eye = iota((NQ, NQ), 0) == iota((NQ, NQ), 1)
    own_f = own_ref[...].astype(f32)
    own_col = jnp.concatenate(
        [
            jnp.sum(jnp.where(eye, own_f[g : g + 1, :], 0.0), axis=1, keepdims=True)
            for g in range(GROUPS)
        ],
        axis=0,
    )
    loc_f = dot_nt(hot(eye), loc_ref[...].astype(f32))
    mask_f = mask_ref[...].astype(f32)
    src_r, dst_c = iota((NQ, 128), 0), iota((NQ, 128), 1)
    places = [hot((src_r == WIDTH * g + dst_c) & (dst_c < WIDTH)) for g in range(GROUPS)]
    loc_w = jnp.concatenate([dot(loc_f, place) for place in places], axis=0)
    mask_w = [dot(mask_f, place) for place in places]
    pair_q = (iota((npair, 128), 0) % NQ).astype(f32)
    loc_w = jnp.where(iota((npair, 128), 1) == WIDTH, pair_q, loc_w)
    ra, ca = iota((npair, npair), 0), iota((npair, npair), 1)
    own_row = jnp.sum(jnp.where(ra == ca, own_col, 0.0), axis=0, keepdims=True)
    same = own_col == own_row
    rank_col = jnp.sum(hot(same & (ca % NQ < ra % NQ)), axis=1, keepdims=True)
    rank_row = jnp.sum(hot(same & (ra % NQ < ca % NQ)), axis=0, keepdims=True)
    slot_col = CAP * own_col + rank_col
    slot_row = CAP * own_row + rank_row
    st = hot(slot_col == iota((npair, SLOTS), 1).astype(f32))
    s_hot = hot(slot_row == iota((SLOTS, npair), 0).astype(f32))
    slot_wide = jnp.sum(
        jnp.where(iota((npair, 128), 0) == iota((npair, 128), 1), slot_col, 0.0),
        axis=0, keepdims=True,
    )
    tbla_v[...] = index(jnp.broadcast_to(slot_wide, (8, 128)), SLOTS)
    tbla_copy = pltpu.make_async_copy(tbla_v, tbla, sem_tbl)
    tbla_copy.start()
    put_rows(m_a, dot(s_hot, loc_w))
    tbla_copy.wait()
    pl.semaphore_wait(barrier, NZ - 1 + NC - 1 + NR - 1)

    first_hop(m_a, m_b, m_sem)

    plus = [q_low, plus1, plus2, plus3, far]
    minus = [q_low, minus1, minus2, minus3, far]
    last_hop = NZ // 2 - 1
    piece = NQ // PIECES

    def pass_on(h, k):
        rows = pl.ds(piece * k, piece)
        if h < last_hop or 2 * k < PIECES:
            to_pool(
                plus[h].at[rows], plus[h + 1].at[rows], hop_s, plus_r.at[PIECES * h + k], along_z(1)
            ).start()
        if h < last_hop or 2 * k >= PIECES:
            to_pool(
                minus[h].at[rows], minus[h + 1].at[rows], hop_s, minus_r.at[PIECES * h + k], along_z(-1)
            ).start()

    def relay(h):
        for k in range(PIECES):
            rows = pl.ds(piece * k, piece)
            wait_bytes(plus[h].at[rows], plus_r.at[PIECES * (h - 1) + k])
            wait_bytes(minus[h].at[rows], minus_r.at[PIECES * (h - 1) + k])
            pass_on(h, k)

    for k in range(PIECES):
        pass_on(0, k)

    second_hop(m_b, m_c, m_sem)
    take_rows(m_b)
    r_i, c_i = iota((128, 128), 0), iota((128, 128), 1)
    picked = jnp.sum(
        jnp.where(r_i == c_i, rows_ref[:, WIDTH : WIDTH + 1], 0.0), axis=0, keepdims=True
    )
    tblm_v[...] = index(jnp.broadcast_to(picked, (8, 128)), NQ)
    tblm_copy = pltpu.make_async_copy(tblm_v, tblm, sem_tbl)
    tblm_copy.start()

    def deliver(block, source):
        for e in range(1, NC):
            target = lax.rem(c + e, NC)
            row = CAP * (NC * source + target)
            for k in range(CAP):
                q_send[row + k] = block[tblm[0, row + k]]
            to_pool(
                q_send.at[pl.ds(row, CAP)],
                q_recv.at[pl.ds(CAP * (NC * source + c), CAP)],
                q_ss, q_rs, NC * z + target,
            ).start()
        row = CAP * (NC * source + c)
        for k in range(CAP):
            q_recv[row + k] = block[tblm[0, row + k]]

    def deliver_both(h):
        deliver(plus[h], lax.rem(z + NZ - h, NZ))
        deliver(minus[h], lax.rem(z + h, NZ))

    def norm_passage(p, _):
        x = p_raw[p].astype(f32)
        inv = lax.rsqrt(jnp.sum(x * x, axis=-1, keepdims=True) + EPSILON)
        p_low[p] = (x * inv).astype(bf16)
        return 0

    relay(1)
    tblm_copy.wait()
    deliver(q_low, z)
    relay(2)
    deliver_both(1)
    relay(3)
    deliver_both(2)
    deliver_both(3)
    p_copy.wait()
    lax.fori_loop(0, NPASS // 2, norm_passage, 0, unroll=2)
    for k in range(PIECES):
        rows = pl.ds(piece * k, piece)
        arrival = plus_r if 2 * k < PIECES else minus_r
        wait_bytes(far.at[rows], arrival.at[PIECES * last_hop + k])
    deliver(far, lax.rem(z + NZ // 2, NZ))

    arrived(m_c, m_sem)
    take_rows(m_c)
    loc_r = rows_ref[...]
    pc, jc, pr, jr = c_i % NPASS, c_i // NPASS, r_i % NPASS, r_i // NPASS
    one_hot = hot(dot(loc_r, hot((r_i == jc) & (r_i < WIDTH))) == pc.astype(f32))
    before = dot(hot(c_i < r_i), one_hot)
    total = jnp.broadcast_to(jnp.sum(one_hot, axis=0, keepdims=True), (8, 128))
    base = dot(total, hot((pr == pc) & (jr < jc)))[0:1, :]
    tiles = jnp.floor((dot(total, hot(pr == pc)) + (TILE - 1)) * (1.0 / TILE))
    offset = dot(tiles, hot((jr == 0) & (pr < pc)))
    rank = base + before
    rank_tile = jnp.floor(rank * (1.0 / TILE))
    x_tile = one_hot * (offset[0:1, :] + rank_tile)
    x_rest = one_hot * (rank - TILE * rank_tile)
    fold = hot((c_i == jr) & (c_i < WIDTH))
    tile_c = dot(x_tile, fold)
    rest_c = dot(x_rest, fold)
    fold_row = hot(iota((8, 128), 0) == iota((8, 128), 1) // NPASS)
    tile_r = dot_nt(fold_row, x_tile)
    rest_r = dot_nt(fold_row, x_rest)
    loc_rows = dot_nt(hot(iota((8, 128), 0) == iota((8, 128), 1)), loc_r)
    sub8 = iota((8, 128), 0).astype(f32)
    slot_ids = iota((8, 128), 1).astype(f32)
    table = jnp.zeros((16, 128), f32)
    for j in range(WIDTH):
        rest_j = rest_r[j : j + 1, :]
        lhs = jnp.concatenate(
            [
                jnp.where(rest_j == sub8, slot_ids, 0.0),
                jnp.where(rest_j == 0.0, loc_rows[j : j + 1, :], jnp.zeros((8, 128), f32)),
            ],
            axis=0,
        )
        rhs = hot(tile_c[:, j : j + 1] == c_i.astype(f32))
        rhs_ref[j] = rhs
        table = table + dot(lhs, rhs)
    tblb_v[0:8, :] = index(table[0:8], SLOTS)
    tblb_v[8:16, :] = index(table[8:16], NPASS)
    tblb_v[16:24, :] = index(TILE * tile_r + rest_r, NTILES * TILE)
    tblb_v[24:32, :] = index(offset + tiles - 1.0, NTILES)
    tblb_v[32:40, :] = index(tiles, 2)
    tblb_copy = pltpu.make_async_copy(tblb_v, tblb, sem_tbl)
    tblb_copy.start()
    lax.fori_loop(NPASS // 2, NPASS, norm_passage, 0, unroll=2)
    tblb_copy.wait()

    wait_bytes(q_recv.at[pl.ds(0, CAP * NZ * (NC - 1))], q_rs)
    ones = jnp.ones((PT, DIM), bf16)
    lane8 = iota((8, 128), 1)

    def forward_tile(t, scores):
        p_tile = p_low[tblb[8, t]]
        q_tile = jnp.concatenate([q_recv[tblb[r, t]] for r in range(TILE)], axis=0)
        sims = lax.dot_general(
            q_tile, p_tile, (((1,), (1,)), ((), ())), preferred_element_type=f32
        )
        soft = jnp.exp2(sims * (math.log2(math.e) / TEMPER)).astype(bf16)
        soft_ref[t] = soft
        both = jnp.dot(
            soft, jnp.concatenate([p_tile, ones], axis=1), preferred_element_type=f32
        )
        sums = both[:, DIM:]
        inv = 1.0 / sums
        a_ref[pl.ds(TILE * t, TILE)] = (both[:, :DIM] * inv).reshape(TILE, QT, DIM)
        qn_ref[t] = q_tile.astype(f32) * inv
        means = (sums * (1.0 / PT)).reshape(TILE, QT // 8, 8, DIM)
        product = means[:, 0]
        for i in range(1, QT // 8):
            product = product * means[:, i]
        logs = jnp.sum(jnp.log(product), axis=1)
        score = TEMPER * (logs + QT * math.log(PT))
        return jnp.where(lane8 == t, score, scores)

    scores = lax.fori_loop(0, NTILES, forward_tile, jnp.zeros((8, 128), f32), unroll=UNROLL)

    sc = jnp.zeros((SLOTS, 128), f32)
    lane_s = iota((SLOTS, 128), 1)
    lane_r = iota((SLOTS, 8), 1).astype(f32)
    for j in range(WIDTH):
        picked = hdot_nt(rhs_ref[j], scores)
        col = jnp.sum(
            jnp.where(rest_c[:, j : j + 1] == lane_r, picked, 0.0), axis=1, keepdims=True
        )
        sc = jnp.where(lane_s == j, col, sc)
    put_rows(s_a, sc)
    first_hop(s_a, s_b, s_sem)
    second_hop(s_b, s_c, s_sem)
    arrived(s_c, s_sem)
    take_rows(s_c)

    own_scores = hdot(st, rows_ref[...])
    lane_q = iota((NQ, 128), 1)
    denom = jnp.zeros((NQ, 1), f32)
    exps = []
    for g in range(GROUPS):
        valid = mask_w[g]
        if g == 0:
            valid = jnp.where(lane_q == 0, 1.0, valid)
        e = jnp.exp(own_scores[NQ * g : NQ * (g + 1), :]) * valid
        exps.append(e)
        denom = denom + jnp.sum(e, axis=1, keepdims=True)
    losses = jnp.log(denom) - own_scores[0:NQ, 0:1]
    loss_ref[...] = jnp.sum(
        jnp.where(iota((NQ, NQ), 0) == iota((NQ, NQ), 1), losses, 0.0), axis=0, keepdims=True
    )
    dscore = [LOSS_SCALE * (e / denom) for e in exps]
    dscore[0] = dscore[0] - jnp.where(lane_q == 0, LOSS_SCALE, 0.0)
    w_slots = hdot(s_hot, jnp.concatenate(dscore, axis=0))
    put_rows(w_a, w_slots)
    first_hop(w_a, w_b, w_sem)
    second_hop(w_b, w_c, w_sem)
    arrived(w_c, w_sem)
    take_rows(w_c)

    w_rows = hdot_nt(hot(iota((8, 128), 0) == iota((8, 128), 1)), rows_ref[...])
    w_tile = jnp.zeros((8, 128), f32)
    for j in range(WIDTH):
        lhs = jnp.where(rest_r[j : j + 1, :] == sub8, w_rows[j : j + 1, :], 0.0)
        w_tile = w_tile + hdot(lhs, rhs_ref[j])
    wt_v[...] = w_tile
    wt_copy = pltpu.make_async_copy(wt_v, wt, sem_tbl)
    wt_copy.start()
    wt_copy.wait()

    def group_grad(s):
        acc = jnp.zeros((QT, DIM), f32)
        for j in range(WIDTH):
            pos = tblb[16 + j, s]
            acc = acc + wt[pos & (TILE - 1), pos >> 3] * a_ref[pos]
        return acc.astype(bf16)

    def send_ret(d, _):
        peer = lax.rem(me + d, NP)
        for k in range(CAP):
            ret_send[CAP * peer + k] = group_grad(CAP * peer + k)
        to_pool(
            ret_send.at[pl.ds(CAP * peer, CAP)], ret_recv.at[pl.ds(CAP * me, CAP)], r_ss, r_rs, peer
        ).start()
        return 0

    lax.fori_loop(1, NP, send_ret, 0)
    for k in range(CAP):
        ret_recv[CAP * me + k] = group_grad(CAP * me + k)

    def passage_tile(t, acc):
        qs = jnp.concatenate(
            [
                (qn_ref[t, QT * r : QT * (r + 1), :] * wt[r, t]).astype(bf16)
                for r in range(TILE)
            ],
            axis=0,
        )
        grad = lax.dot_general(
            qs, soft_ref[t], (((0,), (0,)), ((), ())), preferred_element_type=f32
        )
        halves = jnp.concatenate([grad[:, :128], grad[:, 128:]], axis=0)
        prev = jnp.maximum(t - 1, 0)
        again = (t > 0) & (tblb[8, t] == tblb[8, prev])
        keep = jnp.where(again, 1.0, 0.0).astype(f32)
        acc = halves + keep * acc
        a_ref[pl.ds(TILE * t, TILE)] = acc.reshape(TILE, QT, DIM)
        return acc

    lax.fori_loop(0, NTILES, passage_tile, jnp.zeros((PT, DIM), f32), unroll=UNROLL)

    after, opposite, before_me = (lax.rem(rep + d, NR) for d in (1, 2, 3))

    def to_rep(src, dst, rs, target):
        pltpu.make_async_remote_copy(
            src_ref=src, dst_ref=dst, send_sem=x_ss, recv_sem=rs, device_id=(me, target), device_id_type=MESH
        ).start()

    for chunk in range(NPASS // RS_CHUNK):

        def cut_passage(i, _):
            p = chunk * RS_CHUNK + i
            last = TILE * tblb[24, p]
            used = tblb[32, p].astype(f32)
            for half in range(2):
                x = jnp.concatenate(
                    [a_ref[last + 4 * half + m] for m in range(4)], axis=0
                )
                y = (x * used).T.astype(bf16)
                for part in range(2):
                    rs_send[2 * half + part, p] = y[SHARE * part : SHARE * (part + 1), :]
            return 0

        lax.fori_loop(0, RS_CHUNK, cut_passage, 0, unroll=RS_CHUNK)
        rows = pl.ds(chunk * RS_CHUNK, RS_CHUNK)
        if 2 * chunk * RS_CHUNK < NPASS:
            to_rep(rs_send.at[opposite, rows], via_plus.at[rows], v_rs.at[0], after)
            to_rep(rs_send.at[before_me, rows], rs_recv.at[1, rows], x_rs, before_me)
        else:
            back = pl.ds(chunk * RS_CHUNK - NPASS // 2, RS_CHUNK)
            to_rep(rs_send.at[opposite, rows], via_minus.at[back], v_rs.at[1], before_me)
            to_rep(rs_send.at[after, rows], rs_recv.at[0, rows], x_rs, after)

    low, top = pl.ds(0, NPASS // 2), pl.ds(NPASS // 2, NPASS // 2)
    wait_bytes(via_plus, v_rs.at[0])

    def add_plus(i, _):
        sum_plus[i] = (rs_send[after, i].astype(f32) + via_plus[i].astype(f32)).astype(bf16)
        return 0

    lax.fori_loop(0, NPASS // 2, add_plus, 0, unroll=4)
    to_rep(sum_plus, rs_recv.at[0, low], x_rs, after)
    wait_bytes(via_minus, v_rs.at[1])

    def add_minus(i, _):
        sum_minus[i] = (
            rs_send[before_me, NPASS // 2 + i].astype(f32) + via_minus[i].astype(f32)
        ).astype(bf16)
        return 0

    lax.fori_loop(0, NPASS // 2, add_minus, 0, unroll=4)
    to_rep(sum_minus, rs_recv.at[1, top], x_rs, before_me)

    wait_bytes(ret_recv.at[pl.ds(0, CAP * (NP - 1))], r_rs)

    def sum_query(a, _):
        up = jnp.zeros((QT, DIM), f32)
        for g in range(GROUPS):
            up = up + ret_recv[tbla[0, NQ * g + a]].astype(f32)
        uq_ref[a] = up
        return 0

    lax.fori_loop(0, NQ, sum_query, 0, unroll=4)

    wait_bytes(rs_recv, x_rs)

    def sum_passage(p, _):
        up = rs_send[rep, p].astype(f32)
        for d in range(2):
            up = up + rs_recv[d, p].astype(f32)
        up_ref[p] = up
        return 0

    lax.fori_loop(0, NPASS, sum_passage, 0, unroll=4)

    for send, sems in ((m_a, m_sem), (s_a, s_sem), (w_a, w_sem)):
        wait_bytes(send.at[pl.ds(0, NZ - 1)], sems.at[0])
        wait_bytes(send.at[pl.ds(0, NC - 1)], sems.at[2])
    wait_bytes(q_send.at[pl.ds(0, NQ * (NZ - 1))], hop_s)
    wait_bytes(q_send.at[pl.ds(0, CAP * NZ * (NC - 1))], q_ss)
    wait_bytes(ret_send.at[pl.ds(0, CAP * (NP - 1))], r_ss)
    wait_bytes(rs_send.at[pl.ds(0, NR - 1)], x_ss)


def unit_backward(x, up):
    x = x.astype(f32)
    inv = lax.rsqrt(jnp.sum(x * x, axis=-1, keepdims=True) + EPSILON)
    unit = x * inv
    return inv * (up - unit * jnp.sum(unit * up, axis=-1, keepdims=True))


def finish(loss_in, q_ref, uq_ref, p_any, up_ref, loss_ref, gq_ref, gp_ref, p_share, sem):
    step = pl.program_id(0)

    @pl.when(step == 0)
    def _():
        start = pl.multiple_of(lax.axis_index("rep") * SHARE, SHARE)
        copy = pltpu.make_async_copy(p_any.at[:, pl.ds(start, SHARE)], p_share, sem)
        copy.start()
        loss_ref[...] = loss_in[...]
        for a in range(NQ):
            gq_ref[a] = unit_backward(q_ref[a], uq_ref[a])
        copy.wait()

    for i in range(RS_CHUNK):
        gp_ref[i] = unit_backward(p_share[step * RS_CHUNK + i], up_ref[i])


def per_device(query_vecs, passage_vecs, owner_ids, local_ids, cand_mask):
    vmem = pl.BlockSpec(memory_space=pltpu.VMEM)
    anywhere = pl.BlockSpec(memory_space=pl.ANY)
    rows = pltpu.VMEM((NZ, NC, CAP, 128), f32)
    block = pltpu.VMEM((NQ, QT, DIM), bf16)
    dma = pltpu.SemaphoreType.DMA
    outs = (
        jax.ShapeDtypeStruct((1, NQ), f32),
        jax.ShapeDtypeStruct((NQ, QT, DIM), f32),
        jax.ShapeDtypeStruct((NPASS, SHARE, DIM), f32),
    )
    loss, up_query, up_passage = pl.pallas_call(
        kernel,
        out_shape=outs,
        in_specs=[vmem, anywhere, vmem, vmem, vmem],
        out_specs=[vmem, vmem, vmem],
        scratch_shapes=[
            pltpu.VMEM((NPASS, PT, DIM), bf16),
            pltpu.VMEM((NPASS, PT, DIM), bf16),
        ]
        + [block] * 8
        + [
            pltpu.VMEM((SLOTS, QT, DIM), bf16),
            pltpu.VMEM((SLOTS, QT, DIM), bf16),
        ]
        + [rows] * 9
        + [
            pltpu.VMEM((SLOTS, 128), f32),
            pltpu.VMEM((WIDTH, 128, 128), f32),
            pltpu.VMEM((NTILES, TILE * QT, PT), bf16),
            pltpu.VMEM((NTILES * TILE, QT, DIM), f32),
            pltpu.VMEM((NTILES, TILE * QT, DIM), f32),
            pltpu.VMEM((SLOTS, QT, DIM), bf16),
            pltpu.VMEM((SLOTS, QT, DIM), bf16),
            pltpu.VMEM((NR, NPASS, SHARE, DIM), bf16),
            pltpu.VMEM((2, NPASS, SHARE, DIM), bf16),
        ]
        + [pltpu.VMEM((NPASS // 2, SHARE, DIM), bf16)] * 4
        + [
            pltpu.VMEM((8, 128), i32),
            pltpu.VMEM((8, 128), i32),
            pltpu.VMEM((40, 128), i32),
            pltpu.VMEM((8, 128), f32),
            pltpu.SMEM((8, 128), i32),
            pltpu.SMEM((8, 128), i32),
            pltpu.SMEM((40, 128), i32),
            pltpu.SMEM((8, 128), f32),
        ]
        + [dma(()), dma(()), dma(()), dma((PIECES * NZ // 2,)), dma((PIECES * NZ // 2,)), dma(()), dma(())]
        + [dma((4,))] * 3
        + [dma(())] * 4
        + [dma((2,))],
        compiler_params=pltpu.CompilerParams(
            collective_id=0, has_side_effects=True, vmem_limit_bytes=62 * 1024 * 1024
        ),
    )(
        query_vecs,
        passage_vecs,
        owner_ids.T,
        local_ids.transpose(1, 2, 0).reshape(GROUPS * WIDTH, NQ),
        cand_mask,
    )
    whole = lambda shape: pl.BlockSpec(shape, lambda i: (0,) * len(shape))
    part = pl.BlockSpec((RS_CHUNK, SHARE, DIM), lambda i: (i, 0, 0))
    loss, grad_query, grad_passage = pl.pallas_call(
        finish,
        grid=(NPASS // RS_CHUNK,),
        out_shape=outs,
        in_specs=[whole((1, NQ)), whole((NQ, QT, DIM)), whole((NQ, QT, DIM)), anywhere, part],
        out_specs=[whole((1, NQ)), whole((NQ, QT, DIM)), part],
        scratch_shapes=[pltpu.VMEM((NPASS, SHARE, DIM), bf16), dma(())],
    )(loss, query_vecs, up_query, passage_vecs, up_passage)
    return (loss.reshape(NQ), grad_query, grad_passage)


def solution(mesh):
    return jax.shard_map(
        per_device,
        mesh=mesh,
        in_specs=(
            P(("pool", "rep"), None, None),
            P("pool", None, None),
            P(("pool", "rep"), None),
            P(("pool", "rep"), None, None),
            P(("pool", "rep"), None),
        ),
        out_specs=(P(("pool", "rep")), P(("pool", "rep"), None, None), P("pool", "rep", None)),
        check_vma=False,
    )
```

```python
import math

import jax
import jax.numpy as jnp
from jax import lax
from jax.experimental import pallas as pl
from jax.experimental.pallas import tpu as pltpu
from jax.sharding import PartitionSpec as P

MESH = pl.DeviceIdType.MESH
f32, bf16, i32 = jnp.float32, jnp.bfloat16, jnp.int32

TEMPER = 0.05
LOSS_SCALE = 16.0
EPSILON = 1e-06

NP = 64
NR = 4
NZ = 8
NX = 4
NC = NP // NZ
PIECES = 4
CAP = 2
NQ = 16
QT = 32
DIM = 128
PT = 256
NPASS = 32
GROUPS = 4
WIDTH = 4
SLOTS = NP * CAP
TILE = 8
NTILES = (SLOTS * WIDTH + NPASS * (TILE - 1)) // TILE
SHARE = PT // NR
RS_CHUNK = 8
UNROLL = 23
HIGH = lax.Precision.HIGHEST


def iota(shape, dim):
    return lax.broadcasted_iota(i32, shape, dim)


def hot(cond, dtype=f32):
    return jnp.where(cond, 1.0, 0.0).astype(dtype)


def index(x, bound):
    return jnp.clip(x.astype(i32), 0, bound - 1)


def dot(a, b):
    return jnp.dot(a.astype(bf16), b.astype(bf16), preferred_element_type=f32)


def dot_nt(a, b):
    return lax.dot_general(
        a.astype(bf16), b.astype(bf16), (((1,), (1,)), ((), ())), preferred_element_type=f32
    )


def hdot(a, b):
    return jnp.dot(a, b, preferred_element_type=f32, precision=HIGH)


def hdot_nt(a, b):
    return lax.dot_general(
        a, b, (((1,), (1,)), ((), ())), preferred_element_type=f32, precision=HIGH
    )


def kernel(
    q_ref, p_any, own_ref, loc_ref, mask_ref,
    loss_ref, uq_ref, up_ref,
    p_raw, p_low, q_low, plus1, plus2, plus3, minus1, minus2, minus3, far, q_send, q_recv,
    m_a, m_b, m_c, s_a, s_b, s_c, w_a, w_b, w_c,
    rows_ref, rhs_ref, soft_ref, a_ref, qn_ref, ret_send, ret_recv, rs_send, rs_recv, via_plus, via_minus, sum_plus, sum_minus, q_via, ret_via,
    tbla_v, tblm_v, tblb_v, wt_v, tbla, tblm, tblb, wt,
    sem_p, sem_tbl, hop_s, plus_r, minus_r, q_ss, q_rs, m_sem, s_sem, w_sem, r_ss, r_rs, x_ss, x_rs, v_rs, q_vr, ret_vs, ret_vr,
):
    me = lax.axis_index("pool")
    rep = lax.axis_index("rep")
    z = lax.div(me, NC)
    c = lax.rem(me, NC)
    col, core = lax.div(c, 2), lax.rem(c, 2)

    def wait_bytes(ref, sem):
        pltpu.make_async_copy(ref, ref, sem).wait()

    def to_pool(src, dst, ss, rs, peer):
        return pltpu.make_async_remote_copy(
            src_ref=src, dst_ref=dst, send_sem=ss, recv_sem=rs, device_id=(peer, rep), device_id_type=MESH
        )

    def along_z(e):
        return NC * lax.rem(z + NZ + e, NZ) + c

    def in_plane(e):
        return NC * z + lax.rem(c + e, NC)

    def first_hop(send, mid, sems):
        for e in range(1, NZ):
            target = lax.rem(z + e, NZ)
            to_pool(send.at[target], mid.at[z], sems.at[0], sems.at[1], NC * target + c).start()
        mid[z] = send[z]

    def second_hop(mid, recv, sems):
        wait_bytes(mid.at[pl.ds(0, NZ - 1)], sems.at[1])
        for e in range(1, NC):
            target = lax.rem(c + e, NC)
            to_pool(mid.at[:, target], recv.at[:, c], sems.at[2], sems.at[3], NC * z + target).start()
        for k in range(NZ):
            recv[k, c] = mid[k, c]

    def arrived(recv, sems):
        wait_bytes(recv.at[pl.ds(0, NC - 1)], sems.at[3])

    def put_rows(send, rows):
        for peer in range(NP):
            send[peer // NC, peer % NC] = rows[CAP * peer : CAP * (peer + 1), :]

    def take_rows(recv):
        for peer in range(NP):
            rows_ref[CAP * peer : CAP * (peer + 1), :] = recv[peer // NC, peer % NC]

    p_copy = pltpu.make_async_copy(p_any, p_raw, sem_p)
    p_copy.start()

    barrier = pltpu.get_barrier_semaphore()
    for e in range(1, NZ):
        pl.semaphore_signal(barrier, inc=1, device_id=(along_z(e), rep), device_id_type=MESH)
    for e in range(1, NC):
        pl.semaphore_signal(barrier, inc=1, device_id=(in_plane(e), rep), device_id_type=MESH)
    for d in range(1, NR):
        pl.semaphore_signal(
            barrier, inc=1, device_id=(me, lax.rem(rep + d, NR)), device_id_type=MESH
        )

    for a in range(NQ):
        x = q_ref[a].astype(f32)
        inv = lax.rsqrt(jnp.sum(x * x, axis=-1, keepdims=True) + EPSILON)
        q_low[a] = (x * inv).astype(bf16)

    npair = GROUPS * NQ
    eye = iota((NQ, NQ), 0) == iota((NQ, NQ), 1)
    own_f = own_ref[...].astype(f32)
    own_col = jnp.concatenate(
        [
            jnp.sum(jnp.where(eye, own_f[g : g + 1, :], 0.0), axis=1, keepdims=True)
            for g in range(GROUPS)
        ],
        axis=0,
    )
    loc_f = dot_nt(hot(eye), loc_ref[...].astype(f32))
    mask_f = mask_ref[...].astype(f32)
    src_r, dst_c = iota((NQ, 128), 0), iota((NQ, 128), 1)
    places = [hot((src_r == WIDTH * g + dst_c) & (dst_c < WIDTH)) for g in range(GROUPS)]
    loc_w = jnp.concatenate([dot(loc_f, place) for place in places], axis=0)
    mask_w = [dot(mask_f, place) for place in places]
    pair_q = (iota((npair, 128), 0) % NQ).astype(f32)
    loc_w = jnp.where(iota((npair, 128), 1) == WIDTH, pair_q, loc_w)
    ra, ca = iota((npair, npair), 0), iota((npair, npair), 1)
    own_row = jnp.sum(jnp.where(ra == ca, own_col, 0.0), axis=0, keepdims=True)
    same = own_col == own_row
    rank_col = jnp.sum(hot(same & (ca % NQ < ra % NQ)), axis=1, keepdims=True)
    rank_row = jnp.sum(hot(same & (ra % NQ < ca % NQ)), axis=0, keepdims=True)
    slot_col = CAP * own_col + rank_col
    slot_row = CAP * own_row + rank_row
    st = hot(slot_col == iota((npair, SLOTS), 1).astype(f32))
    s_hot = hot(slot_row == iota((SLOTS, npair), 0).astype(f32))
    slot_wide = jnp.sum(
        jnp.where(iota((npair, 128), 0) == iota((npair, 128), 1), slot_col, 0.0),
        axis=0, keepdims=True,
    )
    tbla_v[...] = index(jnp.broadcast_to(slot_wide, (8, 128)), SLOTS)
    tbla_copy = pltpu.make_async_copy(tbla_v, tbla, sem_tbl)
    tbla_copy.start()
    put_rows(m_a, dot(s_hot, loc_w))
    tbla_copy.wait()
    pl.semaphore_wait(barrier, NZ - 1 + NC - 1 + NR - 1)

    first_hop(m_a, m_b, m_sem)

    plus = [q_low, plus1, plus2, plus3, far]
    minus = [q_low, minus1, minus2, minus3, far]
    last_hop = NZ // 2 - 1
    piece = NQ // PIECES

    def pass_on(h, k):
        rows = pl.ds(piece * k, piece)
        if h < last_hop or 2 * k < PIECES:
            to_pool(
                plus[h].at[rows], plus[h + 1].at[rows], hop_s, plus_r.at[PIECES * h + k], along_z(1)
            ).start()
        if h < last_hop or 2 * k >= PIECES:
            to_pool(
                minus[h].at[rows], minus[h + 1].at[rows], hop_s, minus_r.at[PIECES * h + k], along_z(-1)
            ).start()

    def relay(h):
        for k in range(PIECES):
            rows = pl.ds(piece * k, piece)
            wait_bytes(plus[h].at[rows], plus_r.at[PIECES * (h - 1) + k])
            wait_bytes(minus[h].at[rows], minus_r.at[PIECES * (h - 1) + k])
            pass_on(h, k)

    for k in range(PIECES):
        pass_on(0, k)

    second_hop(m_b, m_c, m_sem)
    take_rows(m_b)
    r_i, c_i = iota((128, 128), 0), iota((128, 128), 1)
    picked = jnp.sum(
        jnp.where(r_i == c_i, rows_ref[:, WIDTH : WIDTH + 1], 0.0), axis=0, keepdims=True
    )
    tblm_v[...] = index(jnp.broadcast_to(picked, (8, 128)), NQ)
    tblm_copy = pltpu.make_async_copy(tblm_v, tblm, sem_tbl)
    tblm_copy.start()

    def chip(dx):
        return 2 * lax.rem(col + NX + dx, NX)

    def deliver(block, source, via=None):
        def fill(target):
            row = CAP * (NC * source + target)
            for k in range(CAP):
                q_send[row + k] = block[tblm[0, row + k]]
            return row

        for dx in (2, 1, 3, 0):
            if dx == 2 and via is not None:
                row = fill(chip(2))
                fill(chip(2) + 1)
                to_pool(
                    q_send.at[pl.ds(row, 2 * CAP)], q_via.at[via], q_ss, q_vr.at[via],
                    NC * z + chip(-1) + core,
                ).start()
                continue
            for dc in range(2):
                if dx == 0 and dc == 0:
                    continue
                target = chip(dx) + lax.rem(core + dc, 2)
                row = fill(target)
                to_pool(
                    q_send.at[pl.ds(row, CAP)],
                    q_recv.at[pl.ds(CAP * (NC * source + c), CAP)],
                    q_ss, q_rs, NC * z + target,
                ).start()
        row = CAP * (NC * source + c)
        for k in range(CAP):
            q_recv[row + k] = block[tblm[0, row + k]]

    def forward_via(via, source):
        wait_bytes(q_via.at[via], q_vr.at[via])
        sender = chip(1) + core
        for k in range(2):
            to_pool(
                q_via.at[via, pl.ds(CAP * k, CAP)],
                q_recv.at[pl.ds(CAP * (NC * source + sender), CAP)],
                q_ss, q_rs, NC * z + chip(-1) + k,
            ).start()

    def ring(dz):
        return lax.rem(z + NZ + dz, NZ)

    def norm_passage(p, _):
        x = p_raw[p].astype(f32)
        inv = lax.rsqrt(jnp.sum(x * x, axis=-1, keepdims=True) + EPSILON)
        p_low[p] = (x * inv).astype(bf16)
        return 0

    relay(1)
    tblm_copy.wait()
    deliver(q_low, z, 0)
    relay(2)
    deliver(plus[1], ring(-1), 1)
    deliver(minus[1], ring(1), 2)
    forward_via(0, z)
    relay(3)
    deliver(plus[2], ring(-2), 3)
    forward_via(1, ring(-1))
    forward_via(2, ring(1))
    deliver(minus[2], ring(2))
    deliver(plus[3], ring(-3))
    forward_via(3, ring(-2))
    deliver(minus[3], ring(3))
    p_copy.wait()
    lax.fori_loop(0, NPASS // 2, norm_passage, 0, unroll=2)
    for k in range(PIECES):
        rows = pl.ds(piece * k, piece)
        arrival = plus_r if 2 * k < PIECES else minus_r
        wait_bytes(far.at[rows], arrival.at[PIECES * last_hop + k])
    deliver(far, lax.rem(z + NZ // 2, NZ))

    arrived(m_c, m_sem)
    take_rows(m_c)
    loc_r = rows_ref[...]
    pc, jc, pr, jr = c_i % NPASS, c_i // NPASS, r_i % NPASS, r_i // NPASS
    one_hot = hot(dot(loc_r, hot((r_i == jc) & (r_i < WIDTH))) == pc.astype(f32))
    before = dot(hot(c_i < r_i), one_hot)
    total = jnp.broadcast_to(jnp.sum(one_hot, axis=0, keepdims=True), (8, 128))
    base = dot(total, hot((pr == pc) & (jr < jc)))[0:1, :]
    tiles = jnp.floor((dot(total, hot(pr == pc)) + (TILE - 1)) * (1.0 / TILE))
    offset = dot(tiles, hot((jr == 0) & (pr < pc)))
    rank = base + before
    rank_tile = jnp.floor(rank * (1.0 / TILE))
    x_tile = one_hot * (offset[0:1, :] + rank_tile)
    x_rest = one_hot * (rank - TILE * rank_tile)
    fold = hot((c_i == jr) & (c_i < WIDTH))
    tile_c = dot(x_tile, fold)
    rest_c = dot(x_rest, fold)
    fold_row = hot(iota((8, 128), 0) == iota((8, 128), 1) // NPASS)
    tile_r = dot_nt(fold_row, x_tile)
    rest_r = dot_nt(fold_row, x_rest)
    loc_rows = dot_nt(hot(iota((8, 128), 0) == iota((8, 128), 1)), loc_r)
    sub8 = iota((8, 128), 0).astype(f32)
    slot_ids = iota((8, 128), 1).astype(f32)
    table = jnp.zeros((16, 128), f32)
    for j in range(WIDTH):
        rest_j = rest_r[j : j + 1, :]
        lhs = jnp.concatenate(
            [
                jnp.where(rest_j == sub8, slot_ids, 0.0),
                jnp.where(rest_j == 0.0, loc_rows[j : j + 1, :], jnp.zeros((8, 128), f32)),
            ],
            axis=0,
        )
        rhs = hot(tile_c[:, j : j + 1] == c_i.astype(f32))
        rhs_ref[j] = rhs
        table = table + dot(lhs, rhs)
    tblb_v[0:8, :] = index(table[0:8], SLOTS)
    tblb_v[8:16, :] = index(table[8:16], NPASS)
    tblb_v[16:24, :] = index(TILE * tile_r + rest_r, NTILES * TILE)
    tblb_v[24:32, :] = index(offset + tiles - 1.0, NTILES)
    tblb_v[32:40, :] = index(tiles, 2)
    tblb_copy = pltpu.make_async_copy(tblb_v, tblb, sem_tbl)
    tblb_copy.start()
    lax.fori_loop(NPASS // 2, NPASS, norm_passage, 0, unroll=2)
    tblb_copy.wait()

    wait_bytes(q_recv.at[pl.ds(0, CAP * NZ * (NC - 1))], q_rs)
    ones = jnp.ones((PT, DIM), bf16)
    lane8 = iota((8, 128), 1)

    def forward_tile(t, scores):
        p_tile = p_low[tblb[8, t]]
        q_tile = jnp.concatenate([q_recv[tblb[r, t]] for r in range(TILE)], axis=0)
        sims = lax.dot_general(
            q_tile, p_tile, (((1,), (1,)), ((), ())), preferred_element_type=f32
        )
        soft = jnp.exp2(sims * (math.log2(math.e) / TEMPER)).astype(bf16)
        soft_ref[t] = soft
        both = jnp.dot(
            soft, jnp.concatenate([p_tile, ones], axis=1), preferred_element_type=f32
        )
        sums = both[:, DIM:]
        inv = 1.0 / sums
        a_ref[pl.ds(TILE * t, TILE)] = (both[:, :DIM] * inv).reshape(TILE, QT, DIM)
        qn_ref[t] = q_tile.astype(f32) * inv
        means = (sums * (1.0 / PT)).reshape(TILE, QT // 8, 8, DIM)
        product = means[:, 0]
        for i in range(1, QT // 8):
            product = product * means[:, i]
        logs = jnp.sum(jnp.log(product), axis=1)
        score = TEMPER * (logs + QT * math.log(PT))
        return jnp.where(lane8 == t, score, scores)

    scores = lax.fori_loop(0, NTILES, forward_tile, jnp.zeros((8, 128), f32), unroll=UNROLL)

    sc = jnp.zeros((SLOTS, 128), f32)
    lane_s = iota((SLOTS, 128), 1)
    lane_r = iota((SLOTS, 8), 1).astype(f32)
    for j in range(WIDTH):
        picked = hdot_nt(rhs_ref[j], scores)
        col = jnp.sum(
            jnp.where(rest_c[:, j : j + 1] == lane_r, picked, 0.0), axis=1, keepdims=True
        )
        sc = jnp.where(lane_s == j, col, sc)
    put_rows(s_a, sc)
    first_hop(s_a, s_b, s_sem)
    second_hop(s_b, s_c, s_sem)
    arrived(s_c, s_sem)
    take_rows(s_c)

    own_scores = hdot(st, rows_ref[...])
    lane_q = iota((NQ, 128), 1)
    denom = jnp.zeros((NQ, 1), f32)
    exps = []
    for g in range(GROUPS):
        valid = mask_w[g]
        if g == 0:
            valid = jnp.where(lane_q == 0, 1.0, valid)
        e = jnp.exp(own_scores[NQ * g : NQ * (g + 1), :]) * valid
        exps.append(e)
        denom = denom + jnp.sum(e, axis=1, keepdims=True)
    losses = jnp.log(denom) - own_scores[0:NQ, 0:1]
    loss_ref[...] = jnp.sum(
        jnp.where(iota((NQ, NQ), 0) == iota((NQ, NQ), 1), losses, 0.0), axis=0, keepdims=True
    )
    dscore = [LOSS_SCALE * (e / denom) for e in exps]
    dscore[0] = dscore[0] - jnp.where(lane_q == 0, LOSS_SCALE, 0.0)
    w_slots = hdot(s_hot, jnp.concatenate(dscore, axis=0))
    put_rows(w_a, w_slots)
    first_hop(w_a, w_b, w_sem)
    second_hop(w_b, w_c, w_sem)
    arrived(w_c, w_sem)
    take_rows(w_c)

    w_rows = hdot_nt(hot(iota((8, 128), 0) == iota((8, 128), 1)), rows_ref[...])
    w_tile = jnp.zeros((8, 128), f32)
    for j in range(WIDTH):
        lhs = jnp.where(rest_r[j : j + 1, :] == sub8, w_rows[j : j + 1, :], 0.0)
        w_tile = w_tile + hdot(lhs, rhs_ref[j])
    wt_v[...] = w_tile
    wt_copy = pltpu.make_async_copy(wt_v, wt, sem_tbl)
    wt_copy.start()
    wt_copy.wait()

    def group_grad(s):
        acc = jnp.zeros((QT, DIM), f32)
        for j in range(WIDTH):
            pos = tblb[16 + j, s]
            acc = acc + wt[pos & (TILE - 1), pos >> 3] * a_ref[pos]
        return acc.astype(bf16)

    def fill_ret(peer):
        for k in range(CAP):
            ret_send[CAP * peer + k] = group_grad(CAP * peer + k)
        return ret_send.at[pl.ds(CAP * peer, CAP)]

    split = NC // 2
    for e in range(split):
        to_pool(
            fill_ret(NC * ring(4) + lax.rem(c + split + e, NC)),
            ret_via.at[pl.ds(CAP * e, CAP)], r_ss, ret_vr, along_z(-2),
        ).start()
    mine = ret_recv.at[pl.ds(CAP * me, CAP)]
    for e in range(split):
        peer = NC * ring(4) + lax.rem(c + e, NC)
        to_pool(fill_ret(peer), mine, r_ss, r_rs, peer).start()

    def send_ret(i, _):
        j = i // NC
        dz = (NZ // 2 - 1 - j // 2) * (1 - 2 * (j % 2))
        peer = NC * ring(dz) + lax.rem(c + 1 + i % NC, NC)
        to_pool(fill_ret(peer), mine, r_ss, r_rs, peer).start()
        return 0

    others = NP - NC - 1
    lax.fori_loop(0, others, send_ret, 0, unroll=5)
    for k in range(CAP):
        ret_recv[CAP * me + k] = group_grad(CAP * me + k)
    wait_bytes(ret_via, ret_vr)
    for e in range(split):
        to_pool(
            ret_via.at[pl.ds(CAP * e, CAP)],
            ret_recv.at[pl.ds(CAP * along_z(2), CAP)],
            ret_vs, r_rs, NC * ring(-2) + lax.rem(c + split + e, NC),
        ).start()

    def passage_tile(t, acc):
        qs = jnp.concatenate(
            [
                (qn_ref[t, QT * r : QT * (r + 1), :] * wt[r, t]).astype(bf16)
                for r in range(TILE)
            ],
            axis=0,
        )
        grad = lax.dot_general(
            qs, soft_ref[t], (((0,), (0,)), ((), ())), preferred_element_type=f32
        )
        halves = jnp.concatenate([grad[:, :128], grad[:, 128:]], axis=0)
        prev = jnp.maximum(t - 1, 0)
        again = (t > 0) & (tblb[8, t] == tblb[8, prev])
        keep = jnp.where(again, 1.0, 0.0).astype(f32)
        acc = halves + keep * acc
        a_ref[pl.ds(TILE * t, TILE)] = acc.reshape(TILE, QT, DIM)
        return acc

    lax.fori_loop(0, NTILES, passage_tile, jnp.zeros((PT, DIM), f32), unroll=UNROLL)

    after, opposite, before_me = (lax.rem(rep + d, NR) for d in (1, 2, 3))

    def to_rep(src, dst, rs, target):
        pltpu.make_async_remote_copy(
            src_ref=src, dst_ref=dst, send_sem=x_ss, recv_sem=rs, device_id=(me, target), device_id_type=MESH
        ).start()

    for chunk in range(NPASS // RS_CHUNK):

        def cut_passage(i, _):
            p = chunk * RS_CHUNK + i
            last = TILE * tblb[24, p]
            used = tblb[32, p].astype(f32)
            for half in range(2):
                x = jnp.concatenate(
                    [a_ref[last + 4 * half + m] for m in range(4)], axis=0
                )
                y = (x * used).T.astype(bf16)
                for part in range(2):
                    rs_send[2 * half + part, p] = y[SHARE * part : SHARE * (part + 1), :]
            return 0

        lax.fori_loop(0, RS_CHUNK, cut_passage, 0, unroll=RS_CHUNK)
        rows = pl.ds(chunk * RS_CHUNK, RS_CHUNK)
        if 2 * chunk * RS_CHUNK < NPASS:
            to_rep(rs_send.at[opposite, rows], via_plus.at[rows], v_rs.at[0], after)
            to_rep(rs_send.at[before_me, rows], rs_recv.at[1, rows], x_rs, before_me)
        else:
            back = pl.ds(chunk * RS_CHUNK - NPASS // 2, RS_CHUNK)
            to_rep(rs_send.at[opposite, rows], via_minus.at[back], v_rs.at[1], before_me)
            to_rep(rs_send.at[after, rows], rs_recv.at[0, rows], x_rs, after)

    low, top = pl.ds(0, NPASS // 2), pl.ds(NPASS // 2, NPASS // 2)
    wait_bytes(via_plus, v_rs.at[0])

    def add_plus(i, _):
        sum_plus[i] = (rs_send[after, i].astype(f32) + via_plus[i].astype(f32)).astype(bf16)
        return 0

    lax.fori_loop(0, NPASS // 2, add_plus, 0, unroll=4)
    to_rep(sum_plus, rs_recv.at[0, low], x_rs, after)
    wait_bytes(via_minus, v_rs.at[1])

    def add_minus(i, _):
        sum_minus[i] = (
            rs_send[before_me, NPASS // 2 + i].astype(f32) + via_minus[i].astype(f32)
        ).astype(bf16)
        return 0

    lax.fori_loop(0, NPASS // 2, add_minus, 0, unroll=4)
    to_rep(sum_minus, rs_recv.at[1, top], x_rs, before_me)

    wait_bytes(ret_recv.at[pl.ds(0, CAP * (NP - 1))], r_rs)

    def sum_query(a, _):
        up = jnp.zeros((QT, DIM), f32)
        for g in range(GROUPS):
            up = up + ret_recv[tbla[0, NQ * g + a]].astype(f32)
        uq_ref[a] = up
        return 0

    lax.fori_loop(0, NQ, sum_query, 0, unroll=4)

    wait_bytes(rs_recv, x_rs)

    def sum_passage(p, _):
        up = rs_send[rep, p].astype(f32)
        for d in range(2):
            up = up + rs_recv[d, p].astype(f32)
        up_ref[p] = up
        return 0

    lax.fori_loop(0, NPASS, sum_passage, 0, unroll=4)

    for send, sems in ((m_a, m_sem), (s_a, s_sem), (w_a, w_sem)):
        wait_bytes(send.at[pl.ds(0, NZ - 1)], sems.at[0])
        wait_bytes(send.at[pl.ds(0, NC - 1)], sems.at[2])
    wait_bytes(q_send.at[pl.ds(0, NQ * (NZ - 1))], hop_s)
    wait_bytes(q_send, q_ss)
    wait_bytes(ret_via, ret_vs)
    wait_bytes(ret_send.at[pl.ds(0, CAP * (NP - 1))], r_ss)
    wait_bytes(rs_send.at[pl.ds(0, NR - 1)], x_ss)


def unit_backward(x, up):
    x = x.astype(f32)
    inv = lax.rsqrt(jnp.sum(x * x, axis=-1, keepdims=True) + EPSILON)
    unit = x * inv
    return inv * (up - unit * jnp.sum(unit * up, axis=-1, keepdims=True))


def finish(loss_in, q_ref, uq_ref, p_any, up_ref, loss_ref, gq_ref, gp_ref, p_share, sem):
    step = pl.program_id(0)

    @pl.when(step == 0)
    def _():
        start = pl.multiple_of(lax.axis_index("rep") * SHARE, SHARE)
        copy = pltpu.make_async_copy(p_any.at[:, pl.ds(start, SHARE)], p_share, sem)
        copy.start()
        loss_ref[...] = loss_in[...]
        for a in range(NQ):
            gq_ref[a] = unit_backward(q_ref[a], uq_ref[a])
        copy.wait()

    for i in range(RS_CHUNK):
        gp_ref[i] = unit_backward(p_share[step * RS_CHUNK + i], up_ref[i])


def per_device(query_vecs, passage_vecs, owner_ids, local_ids, cand_mask):
    vmem = pl.BlockSpec(memory_space=pltpu.VMEM)
    anywhere = pl.BlockSpec(memory_space=pl.ANY)
    rows = pltpu.VMEM((NZ, NC, CAP, 128), f32)
    block = pltpu.VMEM((NQ, QT, DIM), bf16)
    dma = pltpu.SemaphoreType.DMA
    outs = (
        jax.ShapeDtypeStruct((1, NQ), f32),
        jax.ShapeDtypeStruct((NQ, QT, DIM), f32),
        jax.ShapeDtypeStruct((NPASS, SHARE, DIM), f32),
    )
    loss, up_query, up_passage = pl.pallas_call(
        kernel,
        out_shape=outs,
        in_specs=[vmem, anywhere, vmem, vmem, vmem],
        out_specs=[vmem, vmem, vmem],
        scratch_shapes=[
            pltpu.VMEM((NPASS, PT, DIM), bf16),
            pltpu.VMEM((NPASS, PT, DIM), bf16),
        ]
        + [block] * 8
        + [
            pltpu.VMEM((SLOTS, QT, DIM), bf16),
            pltpu.VMEM((SLOTS, QT, DIM), bf16),
        ]
        + [rows] * 9
        + [
            pltpu.VMEM((SLOTS, 128), f32),
            pltpu.VMEM((WIDTH, 128, 128), f32),
            pltpu.VMEM((NTILES, TILE * QT, PT), bf16),
            pltpu.VMEM((NTILES * TILE, QT, DIM), f32),
            pltpu.VMEM((NTILES, TILE * QT, DIM), f32),
            pltpu.VMEM((SLOTS, QT, DIM), bf16),
            pltpu.VMEM((SLOTS, QT, DIM), bf16),
            pltpu.VMEM((NR, NPASS, SHARE, DIM), bf16),
            pltpu.VMEM((2, NPASS, SHARE, DIM), bf16),
        ]
        + [pltpu.VMEM((NPASS // 2, SHARE, DIM), bf16)] * 4
        + [
            pltpu.VMEM((4, 2 * CAP, QT, DIM), bf16),
            pltpu.VMEM((CAP * NC // 2, QT, DIM), bf16),
            pltpu.VMEM((8, 128), i32),
            pltpu.VMEM((8, 128), i32),
            pltpu.VMEM((40, 128), i32),
            pltpu.VMEM((8, 128), f32),
            pltpu.SMEM((8, 128), i32),
            pltpu.SMEM((8, 128), i32),
            pltpu.SMEM((40, 128), i32),
            pltpu.SMEM((8, 128), f32),
        ]
        + [dma(()), dma(()), dma(()), dma((PIECES * NZ // 2,)), dma((PIECES * NZ // 2,)), dma(()), dma(())]
        + [dma((4,))] * 3
        + [dma(())] * 4
        + [dma((2,)), dma((4,)), dma(()), dma(())],
        compiler_params=pltpu.CompilerParams(
            collective_id=0, has_side_effects=True, vmem_limit_bytes=62 * 1024 * 1024
        ),
    )(
        query_vecs,
        passage_vecs,
        owner_ids.T,
        local_ids.transpose(1, 2, 0).reshape(GROUPS * WIDTH, NQ),
        cand_mask,
    )
    whole = lambda shape: pl.BlockSpec(shape, lambda i: (0,) * len(shape))
    part = pl.BlockSpec((RS_CHUNK, SHARE, DIM), lambda i: (i, 0, 0))
    loss, grad_query, grad_passage = pl.pallas_call(
        finish,
        grid=(NPASS // RS_CHUNK,),
        out_shape=outs,
        in_specs=[whole((1, NQ)), whole((NQ, QT, DIM)), whole((NQ, QT, DIM)), anywhere, part],
        out_specs=[whole((1, NQ)), whole((NQ, QT, DIM)), part],
        scratch_shapes=[pltpu.VMEM((NPASS, SHARE, DIM), bf16), dma(())],
    )(loss, query_vecs, up_query, passage_vecs, up_passage)
    return (loss.reshape(NQ), grad_query, grad_passage)


def solution(mesh):
    return jax.shard_map(
        per_device,
        mesh=mesh,
        in_specs=(
            P(("pool", "rep"), None, None),
            P("pool", None, None),
            P(("pool", "rep"), None),
            P(("pool", "rep"), None, None),
            P(("pool", "rep"), None),
        ),
        out_specs=(P(("pool", "rep")), P(("pool", "rep"), None, None), P("pool", "rep", None)),
        check_vma=False,
    )
```

```python
import math

import jax
import jax.numpy as jnp
from jax import lax
from jax.experimental import pallas as pl
from jax.experimental.pallas import tpu as pltpu
from jax.sharding import PartitionSpec as P

MESH = pl.DeviceIdType.MESH
f32, bf16, i32 = jnp.float32, jnp.bfloat16, jnp.int32

TEMPER = 0.05
LOSS_SCALE = 16.0
EPSILON = 1e-06

NP = 64
NR = 4
NZ = 8
NC = NP // NZ
PIECES = 4
CAP = 2
NQ = 16
QT = 32
DIM = 128
PT = 256
NPASS = 32
GROUPS = 4
WIDTH = 4
SLOTS = NP * CAP
QUERY, GROUP_SLOTS = WIDTH, WIDTH + 1
FLAGS, FIRST = GROUP_SLOTS + GROUPS, GROUP_SLOTS + GROUPS + WIDTH
TILE = 8
NTILES = (SLOTS * WIDTH + NPASS * (TILE - 1)) // TILE
SHARE = PT // NR
RS_CHUNK = 8
UNROLL = 23
HIGH = lax.Precision.HIGHEST


def iota(shape, dim):
    return lax.broadcasted_iota(i32, shape, dim)


def hot(cond, dtype=f32):
    return jnp.where(cond, 1.0, 0.0).astype(dtype)


def index(x, bound):
    return jnp.clip(x.astype(i32), 0, bound - 1)


def dot(a, b):
    return jnp.dot(a.astype(bf16), b.astype(bf16), preferred_element_type=f32)


def dot_nt(a, b):
    return lax.dot_general(
        a.astype(bf16), b.astype(bf16), (((1,), (1,)), ((), ())), preferred_element_type=f32
    )


def hdot(a, b):
    return jnp.dot(a, b, preferred_element_type=f32, precision=HIGH)


def hdot_nt(a, b):
    return lax.dot_general(
        a, b, (((1,), (1,)), ((), ())), preferred_element_type=f32, precision=HIGH
    )


def kernel(
    q_ref, p_any, own_ref, loc_ref, mask_ref,
    loss_ref, uq_ref, up_ref,
    p_raw, p_low, q_low, plus1, plus2, plus3, minus1, minus2, minus3, far, q_send, q_recv,
    m_a, m_b, m_c, s_a, s_b, s_c,
    rows_ref, rhs_ref, soft_ref, a_ref, qn_ref, ret_send, ret_recv, rs_send, rs_recv, via_plus, via_minus, sum_plus, sum_minus,
    tbla_v, tblm_v, tblb_v, wt_v, tbla, tblm, tblb, wt,
    sem_p, sem_tbl, hop_s, plus_r, minus_r, q_ss, q_rs, m_sem, s_sem, r_ss, r_rs, x_ss, x_rs, v_rs,
):
    me = lax.axis_index("pool")
    rep = lax.axis_index("rep")
    z = lax.div(me, NC)
    c = lax.rem(me, NC)

    def wait_bytes(ref, sem):
        pltpu.make_async_copy(ref, ref, sem).wait()

    def to_pool(src, dst, ss, rs, peer):
        return pltpu.make_async_remote_copy(
            src_ref=src, dst_ref=dst, send_sem=ss, recv_sem=rs, device_id=(peer, rep), device_id_type=MESH
        )

    def along_z(e):
        return NC * lax.rem(z + NZ + e, NZ) + c

    def in_plane(e):
        return NC * z + lax.rem(c + e, NC)

    def first_hop(send, mid, sems):
        for e in range(1, NZ):
            target = lax.rem(z + e, NZ)
            to_pool(send.at[target], mid.at[z], sems.at[0], sems.at[1], NC * target + c).start()
        mid[z] = send[z]

    def second_hop(mid, recv, sems):
        wait_bytes(mid.at[pl.ds(0, NZ - 1)], sems.at[1])
        for e in range(1, NC):
            target = lax.rem(c + e, NC)
            to_pool(mid.at[:, target], recv.at[:, c], sems.at[2], sems.at[3], NC * z + target).start()
        for k in range(NZ):
            recv[k, c] = mid[k, c]

    def arrived(recv, sems):
        wait_bytes(recv.at[pl.ds(0, NC - 1)], sems.at[3])

    def put_rows(send, rows):
        for peer in range(NP):
            send[peer // NC, peer % NC] = rows[CAP * peer : CAP * (peer + 1), :]

    def take_rows(recv):
        for peer in range(NP):
            rows_ref[CAP * peer : CAP * (peer + 1), :] = recv[peer // NC, peer % NC]

    p_copy = pltpu.make_async_copy(p_any, p_raw, sem_p)
    p_copy.start()

    barrier = pltpu.get_barrier_semaphore()
    for e in range(1, NZ):
        pl.semaphore_signal(barrier, inc=1, device_id=(along_z(e), rep), device_id_type=MESH)
    for e in range(1, NC):
        pl.semaphore_signal(barrier, inc=1, device_id=(in_plane(e), rep), device_id_type=MESH)
    for d in range(1, NR):
        pl.semaphore_signal(
            barrier, inc=1, device_id=(me, lax.rem(rep + d, NR)), device_id_type=MESH
        )

    for a in range(NQ):
        x = q_ref[a].astype(f32)
        inv = lax.rsqrt(jnp.sum(x * x, axis=-1, keepdims=True) + EPSILON)
        q_low[a] = (x * inv).astype(bf16)

    npair = GROUPS * NQ
    eye = iota((NQ, NQ), 0) == iota((NQ, NQ), 1)
    own_f = own_ref[...].astype(f32)
    own_col = jnp.concatenate(
        [
            jnp.sum(jnp.where(eye, own_f[g : g + 1, :], 0.0), axis=1, keepdims=True)
            for g in range(GROUPS)
        ],
        axis=0,
    )
    loc_f = dot_nt(hot(eye), loc_ref[...].astype(f32))
    mask_f = mask_ref[...].astype(f32)
    src_r, dst_c = iota((NQ, 128), 0), iota((NQ, 128), 1)
    places = [hot((src_r == WIDTH * g + dst_c) & (dst_c < WIDTH)) for g in range(GROUPS)]
    shifted = [
        hot((src_r == WIDTH * g + dst_c - FLAGS) & (dst_c >= FLAGS) & (dst_c < FLAGS + WIDTH))
        for g in range(GROUPS)
    ]
    loc_w = jnp.concatenate([dot(loc_f, place) for place in places], axis=0)
    ra, ca = iota((npair, npair), 0), iota((npair, npair), 1)
    own_row = jnp.sum(jnp.where(ra == ca, own_col, 0.0), axis=0, keepdims=True)
    same = own_col == own_row
    rank_col = jnp.sum(hot(same & (ca % NQ < ra % NQ)), axis=1, keepdims=True)
    rank_row = jnp.sum(hot(same & (ra % NQ < ca % NQ)), axis=0, keepdims=True)
    slot_col = CAP * own_col + rank_col
    slot_row = CAP * own_row + rank_row
    st = hot(slot_col == iota((npair, SLOTS), 1).astype(f32))
    s_hot = hot(slot_row == iota((SLOTS, npair), 0).astype(f32))
    slot_wide = jnp.sum(
        jnp.where(iota((npair, 128), 0) == iota((npair, 128), 1), slot_col, 0.0),
        axis=0, keepdims=True,
    )
    tbla_v[...] = index(jnp.broadcast_to(slot_wide, (8, 128)), SLOTS)
    tbla_copy = pltpu.make_async_copy(tbla_v, tbla, sem_tbl)
    tbla_copy.start()
    lane_q = iota((NQ, 128), 1)
    group_slots = jnp.zeros((NQ, 128), f32)
    for g in range(GROUPS):
        group_slots = jnp.where(lane_q == GROUP_SLOTS + g, slot_col[NQ * g : NQ * (g + 1)], group_slots)
    flags = [dot(mask_f, place) for place in shifted]
    flags[0] = jnp.where((lane_q == FLAGS) | (lane_q == FIRST), 1.0, flags[0])
    lane_n = iota((npair, 128), 1)
    pair_rows = loc_w + jnp.concatenate([group_slots + f for f in flags], axis=0)
    pair_rows = jnp.where(lane_n == QUERY, (iota((npair, 128), 0) % NQ).astype(f32), pair_rows)
    put_rows(m_a, dot(s_hot, pair_rows))
    tbla_copy.wait()
    pl.semaphore_wait(barrier, NZ - 1 + NC - 1 + NR - 1)

    first_hop(m_a, m_b, m_sem)

    plus = [q_low, plus1, plus2, plus3, far]
    minus = [q_low, minus1, minus2, minus3, far]
    last_hop = NZ // 2 - 1
    piece = NQ // PIECES

    def pass_on(h, k):
        rows = pl.ds(piece * k, piece)
        if h < last_hop or 2 * k < PIECES:
            to_pool(
                plus[h].at[rows], plus[h + 1].at[rows], hop_s, plus_r.at[PIECES * h + k], along_z(1)
            ).start()
        if h < last_hop or 2 * k >= PIECES:
            to_pool(
                minus[h].at[rows], minus[h + 1].at[rows], hop_s, minus_r.at[PIECES * h + k], along_z(-1)
            ).start()

    def relay(h):
        for k in range(PIECES):
            rows = pl.ds(piece * k, piece)
            wait_bytes(plus[h].at[rows], plus_r.at[PIECES * (h - 1) + k])
            wait_bytes(minus[h].at[rows], minus_r.at[PIECES * (h - 1) + k])
            pass_on(h, k)

    for k in range(PIECES):
        pass_on(0, k)

    second_hop(m_b, m_c, m_sem)
    take_rows(m_b)
    r_i, c_i = iota((128, 128), 0), iota((128, 128), 1)
    picked = jnp.sum(
        jnp.where(r_i == c_i, rows_ref[:, QUERY : QUERY + 1], 0.0), axis=0, keepdims=True
    )
    tblm_v[...] = index(jnp.broadcast_to(picked, (8, 128)), NQ)
    tblm_copy = pltpu.make_async_copy(tblm_v, tblm, sem_tbl)
    tblm_copy.start()

    def deliver(block, source):
        for e in range(1, NC):
            target = lax.rem(c + e, NC)
            row = CAP * (NC * source + target)
            for k in range(CAP):
                q_send[row + k] = block[tblm[0, row + k]]
            to_pool(
                q_send.at[pl.ds(row, CAP)],
                q_recv.at[pl.ds(CAP * (NC * source + c), CAP)],
                q_ss, q_rs, NC * z + target,
            ).start()
        row = CAP * (NC * source + c)
        for k in range(CAP):
            q_recv[row + k] = block[tblm[0, row + k]]

    def deliver_both(h):
        deliver(plus[h], lax.rem(z + NZ - h, NZ))
        deliver(minus[h], lax.rem(z + h, NZ))

    def norm_passage(p, _):
        x = p_raw[p].astype(f32)
        inv = lax.rsqrt(jnp.sum(x * x, axis=-1, keepdims=True) + EPSILON)
        p_low[p] = (x * inv).astype(bf16)
        return 0

    relay(1)
    tblm_copy.wait()
    deliver(q_low, z)
    relay(2)
    deliver_both(1)
    relay(3)
    deliver_both(2)
    deliver_both(3)
    p_copy.wait()
    lax.fori_loop(0, NPASS // 2, norm_passage, 0, unroll=2)
    for k in range(PIECES):
        rows = pl.ds(piece * k, piece)
        arrival = plus_r if 2 * k < PIECES else minus_r
        wait_bytes(far.at[rows], arrival.at[PIECES * last_hop + k])
    deliver(far, lax.rem(z + NZ // 2, NZ))

    arrived(m_c, m_sem)
    take_rows(m_c)
    loc_r = rows_ref[...]
    pc, jc, pr, jr = c_i % NPASS, c_i // NPASS, r_i % NPASS, r_i // NPASS
    one_hot = hot(dot(loc_r, hot((r_i == jc) & (r_i < WIDTH))) == pc.astype(f32))
    before = dot(hot(c_i < r_i), one_hot)
    total = jnp.broadcast_to(jnp.sum(one_hot, axis=0, keepdims=True), (8, 128))
    base = dot(total, hot((pr == pc) & (jr < jc)))[0:1, :]
    tiles = jnp.floor((dot(total, hot(pr == pc)) + (TILE - 1)) * (1.0 / TILE))
    offset = dot(tiles, hot((jr == 0) & (pr < pc)))
    rank = base + before
    rank_tile = jnp.floor(rank * (1.0 / TILE))
    x_tile = one_hot * (offset[0:1, :] + rank_tile)
    x_rest = one_hot * (rank - TILE * rank_tile)
    fold = hot((c_i == jr) & (c_i < WIDTH))
    tile_c = dot(x_tile, fold)
    rest_c = dot(x_rest, fold)
    fold_row = hot(iota((8, 128), 0) == iota((8, 128), 1) // NPASS)
    tile_r = dot_nt(fold_row, x_tile)
    rest_r = dot_nt(fold_row, x_rest)
    loc_rows = dot_nt(hot(iota((8, 128), 0) == iota((8, 128), 1)), loc_r)
    slot_rows = dot_nt(hot(iota((8, 128), 0) + GROUP_SLOTS == iota((8, 128), 1)), loc_r)
    valid_c = dot(loc_r, hot((r_i == c_i + FLAGS) & (c_i < WIDTH)))
    first_row = dot_nt(hot(iota((8, 128), 1) == FIRST), loc_r)[0:1, :]
    sub8 = iota((8, 128), 0).astype(f32)
    slot_ids = iota((8, 128), 1).astype(f32)
    table = jnp.zeros((16, 128), f32)
    for j in range(WIDTH):
        rest_j = rest_r[j : j + 1, :]
        lhs = jnp.concatenate(
            [
                jnp.where(rest_j == sub8, slot_ids, 0.0),
                jnp.where(rest_j == 0.0, loc_rows[j : j + 1, :], jnp.zeros((8, 128), f32)),
            ],
            axis=0,
        )
        rhs = hot(tile_c[:, j : j + 1] == c_i.astype(f32))
        rhs_ref[j] = rhs
        table = table + dot(lhs, rhs)
    tblb_v[0:8, :] = index(table[0:8], SLOTS)
    tblb_v[8:16, :] = index(table[8:16], NPASS)
    tblb_v[16:24, :] = index(TILE * tile_r + rest_r, NTILES * TILE)
    tblb_v[24:32, :] = index(offset + tiles - 1.0, NTILES)
    tblb_v[32:40, :] = index(tiles, 2)
    tblb_copy = pltpu.make_async_copy(tblb_v, tblb, sem_tbl)
    tblb_copy.start()
    lax.fori_loop(NPASS // 2, NPASS, norm_passage, 0, unroll=2)
    tblb_copy.wait()

    wait_bytes(q_recv.at[pl.ds(0, CAP * NZ * (NC - 1))], q_rs)
    ones = jnp.ones((PT, DIM), bf16)
    lane8 = iota((8, 128), 1)

    def forward_tile(t, scores):
        p_tile = p_low[tblb[8, t]]
        q_tile = jnp.concatenate([q_recv[tblb[r, t]] for r in range(TILE)], axis=0)
        sims = lax.dot_general(
            q_tile, p_tile, (((1,), (1,)), ((), ())), preferred_element_type=f32
        )
        soft = jnp.exp2(sims * (math.log2(math.e) / TEMPER)).astype(bf16)
        soft_ref[t] = soft
        both = jnp.dot(
            soft, jnp.concatenate([p_tile, ones], axis=1), preferred_element_type=f32
        )
        sums = both[:, DIM:]
        inv = 1.0 / sums
        a_ref[pl.ds(TILE * t, TILE)] = (both[:, :DIM] * inv).reshape(TILE, QT, DIM)
        qn_ref[t] = q_tile.astype(f32) * inv
        means = (sums * (1.0 / PT)).reshape(TILE, QT // 8, 8, DIM)
        product = means[:, 0]
        for i in range(1, QT // 8):
            product = product * means[:, i]
        logs = jnp.sum(jnp.log(product), axis=1)
        score = TEMPER * (logs + QT * math.log(PT))
        return jnp.where(lane8 == t, score, scores)

    scores = lax.fori_loop(0, NTILES, forward_tile, jnp.zeros((8, 128), f32), unroll=UNROLL)

    sc = jnp.zeros((SLOTS, 128), f32)
    lane_s = iota((SLOTS, 128), 1)
    lane_r = iota((SLOTS, 8), 1).astype(f32)
    for j in range(WIDTH):
        picked = hdot_nt(rhs_ref[j], scores)
        col = jnp.sum(
            jnp.where(rest_c[:, j : j + 1] == lane_r, picked, 0.0), axis=1, keepdims=True
        )
        sc = jnp.where(lane_s == j, col, sc)
    exps = jnp.exp(sc) * valid_c
    diag = r_i == c_i
    part = jnp.sum(exps, axis=1, keepdims=True)
    s_a[0:1, :] = jnp.sum(jnp.where(diag, part, 0.0), axis=0, keepdims=True)
    s_a[1:2, :] = jnp.sum(jnp.where(diag, sc[:, 0:1], 0.0), axis=0, keepdims=True)
    for e in range(1, NZ):
        to_pool(s_a, s_b.at[z], s_sem.at[0], s_sem.at[1], along_z(e)).start()
    s_b[z] = s_a[...]
    exp_rows = hdot_nt(hot(iota((8, 128), 0) == iota((8, 128), 1)), exps)
    wait_bytes(s_b.at[pl.ds(0, NZ - 1)], s_sem.at[1])
    for e in range(1, NC):
        to_pool(s_b, s_c.at[c], s_sem.at[2], s_sem.at[3], in_plane(e)).start()
    s_c[c] = s_b[...]
    wait_bytes(s_c.at[pl.ds(0, NC - 1)], s_sem.at[3])
    for peer in range(NP):
        rows_ref[CAP * peer : CAP * (peer + 1), :] = s_c[peer % NC, peer // NC]

    sums = rows_ref[...]
    twin = jnp.where(c_i % 2 == 0, pltpu.roll(sums, 127, 1), pltpu.roll(sums, 1, 1))
    denom = jnp.zeros((1, 128), f32)
    odd_lane = (iota((1, 128), 1) % 2).astype(f32)
    for g in range(GROUPS):
        target = slot_rows[g : g + 1, :]
        odd = target - 2.0 * jnp.floor(target * 0.5)
        value = jnp.where(odd == odd_lane, sums, twin)
        denom = denom + jnp.sum(
            jnp.where(r_i.astype(f32) == target - odd, value, 0.0), axis=0, keepdims=True
        )
    denom = jnp.where(denom > 0.0, denom, 1.0)
    w_rows = LOSS_SCALE * (
        exp_rows / denom - jnp.where(iota((8, 128), 0) == 0, first_row, 0.0)
    )

    w_tile = jnp.zeros((8, 128), f32)
    for j in range(WIDTH):
        lhs = jnp.where(rest_r[j : j + 1, :] == sub8, w_rows[j : j + 1, :], 0.0)
        w_tile = w_tile + hdot(lhs, rhs_ref[j])
    wt_v[...] = w_tile
    wt_copy = pltpu.make_async_copy(wt_v, wt, sem_tbl)
    wt_copy.start()
    wt_copy.wait()

    def group_grad(s):
        acc = jnp.zeros((QT, DIM), f32)
        for j in range(WIDTH):
            pos = tblb[16 + j, s]
            acc = acc + wt[pos & (TILE - 1), pos >> 3] * a_ref[pos]
        return acc.astype(bf16)

    def send_ret(d, _):
        peer = lax.rem(me + d, NP)
        for k in range(CAP):
            ret_send[CAP * peer + k] = group_grad(CAP * peer + k)
        to_pool(
            ret_send.at[pl.ds(CAP * peer, CAP)], ret_recv.at[pl.ds(CAP * me, CAP)], r_ss, r_rs, peer
        ).start()
        return 0

    lax.fori_loop(1, NP, send_ret, 0)
    for k in range(CAP):
        ret_recv[CAP * me + k] = group_grad(CAP * me + k)

    odd = slot_col - 2.0 * jnp.floor(slot_col * 0.5)
    own_rows = [
        jnp.sum(
            jnp.where(
                diag,
                jnp.sum(jnp.where(c_i == CAP * me + k, sums, 0.0), axis=1, keepdims=True),
                0.0,
            ),
            axis=0, keepdims=True,
        )
        for k in range(CAP)
    ]
    own = jnp.where(odd == 0.0, own_rows[0], own_rows[1])
    lane_f = iota((npair, 128), 1).astype(f32)
    pair_sum = jnp.sum(jnp.where(lane_f == slot_col - odd, own, 0.0), axis=1, keepdims=True)
    pair_score = jnp.sum(jnp.where(lane_f == slot_col - odd + 1.0, own, 0.0), axis=1, keepdims=True)
    total_sum = pair_sum[0:NQ]
    for g in range(1, GROUPS):
        total_sum = total_sum + pair_sum[NQ * g : NQ * (g + 1)]
    losses = jnp.log(total_sum) - pair_score[0:NQ]
    loss_ref[...] = jnp.sum(jnp.where(eye, losses, 0.0), axis=0, keepdims=True)

    def passage_tile(t, acc):
        qs = jnp.concatenate(
            [
                (qn_ref[t, QT * r : QT * (r + 1), :] * wt[r, t]).astype(bf16)
                for r in range(TILE)
            ],
            axis=0,
        )
        grad = lax.dot_general(
            qs, soft_ref[t], (((0,), (0,)), ((), ())), preferred_element_type=f32
        )
        halves = jnp.concatenate([grad[:, :128], grad[:, 128:]], axis=0)
        prev = jnp.maximum(t - 1, 0)
        again = (t > 0) & (tblb[8, t] == tblb[8, prev])
        keep = jnp.where(again, 1.0, 0.0).astype(f32)
        acc = halves + keep * acc
        a_ref[pl.ds(TILE * t, TILE)] = acc.reshape(TILE, QT, DIM)
        return acc

    lax.fori_loop(0, NTILES, passage_tile, jnp.zeros((PT, DIM), f32), unroll=UNROLL)

    after, opposite, before_me = (lax.rem(rep + d, NR) for d in (1, 2, 3))

    def to_rep(src, dst, rs, target):
        pltpu.make_async_remote_copy(
            src_ref=src, dst_ref=dst, send_sem=x_ss, recv_sem=rs, device_id=(me, target), device_id_type=MESH
        ).start()

    for chunk in range(NPASS // RS_CHUNK):

        def cut_passage(i, _):
            p = chunk * RS_CHUNK + i
            last = TILE * tblb[24, p]
            used = tblb[32, p].astype(f32)
            for half in range(2):
                x = jnp.concatenate(
                    [a_ref[last + 4 * half + m] for m in range(4)], axis=0
                )
                y = (x * used).T.astype(bf16)
                for part in range(2):
                    rs_send[2 * half + part, p] = y[SHARE * part : SHARE * (part + 1), :]
            return 0

        lax.fori_loop(0, RS_CHUNK, cut_passage, 0, unroll=RS_CHUNK)
        rows = pl.ds(chunk * RS_CHUNK, RS_CHUNK)
        if 2 * chunk * RS_CHUNK < NPASS:
            to_rep(rs_send.at[opposite, rows], via_plus.at[rows], v_rs.at[0], after)
            to_rep(rs_send.at[before_me, rows], rs_recv.at[1, rows], x_rs, before_me)
        else:
            back = pl.ds(chunk * RS_CHUNK - NPASS // 2, RS_CHUNK)
            to_rep(rs_send.at[opposite, rows], via_minus.at[back], v_rs.at[1], before_me)
            to_rep(rs_send.at[after, rows], rs_recv.at[0, rows], x_rs, after)

    low, top = pl.ds(0, NPASS // 2), pl.ds(NPASS // 2, NPASS // 2)
    wait_bytes(via_plus, v_rs.at[0])

    def add_plus(i, _):
        sum_plus[i] = (rs_send[after, i].astype(f32) + via_plus[i].astype(f32)).astype(bf16)
        return 0

    lax.fori_loop(0, NPASS // 2, add_plus, 0, unroll=4)
    to_rep(sum_plus, rs_recv.at[0, low], x_rs, after)
    wait_bytes(via_minus, v_rs.at[1])

    def add_minus(i, _):
        sum_minus[i] = (
            rs_send[before_me, NPASS // 2 + i].astype(f32) + via_minus[i].astype(f32)
        ).astype(bf16)
        return 0

    lax.fori_loop(0, NPASS // 2, add_minus, 0, unroll=4)
    to_rep(sum_minus, rs_recv.at[1, top], x_rs, before_me)

    wait_bytes(ret_recv.at[pl.ds(0, CAP * (NP - 1))], r_rs)

    def sum_query(a, _):
        up = jnp.zeros((QT, DIM), f32)
        for g in range(GROUPS):
            up = up + ret_recv[tbla[0, NQ * g + a]].astype(f32)
        uq_ref[a] = up
        return 0

    lax.fori_loop(0, NQ, sum_query, 0, unroll=4)

    wait_bytes(rs_recv, x_rs)

    def sum_passage(p, _):
        up = rs_send[rep, p].astype(f32)
        for d in range(2):
            up = up + rs_recv[d, p].astype(f32)
        up_ref[p] = up
        return 0

    lax.fori_loop(0, NPASS, sum_passage, 0, unroll=4)

    wait_bytes(m_a.at[pl.ds(0, NZ - 1)], m_sem.at[0])
    wait_bytes(m_a.at[pl.ds(0, NC - 1)], m_sem.at[2])
    wait_bytes(s_b.at[pl.ds(0, NZ - 1)], s_sem.at[0])
    wait_bytes(s_c.at[pl.ds(0, NC - 1)], s_sem.at[2])
    wait_bytes(q_send.at[pl.ds(0, NQ * (NZ - 1))], hop_s)
    wait_bytes(q_send.at[pl.ds(0, CAP * NZ * (NC - 1))], q_ss)
    wait_bytes(ret_send.at[pl.ds(0, CAP * (NP - 1))], r_ss)
    wait_bytes(rs_send.at[pl.ds(0, NR - 1)], x_ss)


def unit_backward(x, up):
    x = x.astype(f32)
    inv = lax.rsqrt(jnp.sum(x * x, axis=-1, keepdims=True) + EPSILON)
    unit = x * inv
    return inv * (up - unit * jnp.sum(unit * up, axis=-1, keepdims=True))


def finish(loss_in, q_ref, uq_ref, p_any, up_ref, loss_ref, gq_ref, gp_ref, p_share, sem):
    step = pl.program_id(0)

    @pl.when(step == 0)
    def _():
        start = pl.multiple_of(lax.axis_index("rep") * SHARE, SHARE)
        copy = pltpu.make_async_copy(p_any.at[:, pl.ds(start, SHARE)], p_share, sem)
        copy.start()
        loss_ref[...] = loss_in[...]
        for a in range(NQ):
            gq_ref[a] = unit_backward(q_ref[a], uq_ref[a])
        copy.wait()

    for i in range(RS_CHUNK):
        gp_ref[i] = unit_backward(p_share[step * RS_CHUNK + i], up_ref[i])


def per_device(query_vecs, passage_vecs, owner_ids, local_ids, cand_mask):
    vmem = pl.BlockSpec(memory_space=pltpu.VMEM)
    anywhere = pl.BlockSpec(memory_space=pl.ANY)
    rows = pltpu.VMEM((NZ, NC, CAP, 128), f32)
    block = pltpu.VMEM((NQ, QT, DIM), bf16)
    dma = pltpu.SemaphoreType.DMA
    outs = (
        jax.ShapeDtypeStruct((1, NQ), f32),
        jax.ShapeDtypeStruct((NQ, QT, DIM), f32),
        jax.ShapeDtypeStruct((NPASS, SHARE, DIM), f32),
    )
    loss, up_query, up_passage = pl.pallas_call(
        kernel,
        out_shape=outs,
        in_specs=[vmem, anywhere, vmem, vmem, vmem],
        out_specs=[vmem, vmem, vmem],
        scratch_shapes=[
            pltpu.VMEM((NPASS, PT, DIM), bf16),
            pltpu.VMEM((NPASS, PT, DIM), bf16),
        ]
        + [block] * 8
        + [
            pltpu.VMEM((SLOTS, QT, DIM), bf16),
            pltpu.VMEM((SLOTS, QT, DIM), bf16),
        ]
        + [rows] * 3
        + [
            pltpu.VMEM((CAP, 128), f32),
            pltpu.VMEM((NZ, CAP, 128), f32),
            pltpu.VMEM((NC, NZ, CAP, 128), f32),
            pltpu.VMEM((SLOTS, 128), f32),
            pltpu.VMEM((WIDTH, 128, 128), f32),
            pltpu.VMEM((NTILES, TILE * QT, PT), bf16),
            pltpu.VMEM((NTILES * TILE, QT, DIM), f32),
            pltpu.VMEM((NTILES, TILE * QT, DIM), f32),
            pltpu.VMEM((SLOTS, QT, DIM), bf16),
            pltpu.VMEM((SLOTS, QT, DIM), bf16),
            pltpu.VMEM((NR, NPASS, SHARE, DIM), bf16),
            pltpu.VMEM((2, NPASS, SHARE, DIM), bf16),
        ]
        + [pltpu.VMEM((NPASS // 2, SHARE, DIM), bf16)] * 4
        + [
            pltpu.VMEM((8, 128), i32),
            pltpu.VMEM((8, 128), i32),
            pltpu.VMEM((40, 128), i32),
            pltpu.VMEM((8, 128), f32),
            pltpu.SMEM((8, 128), i32),
            pltpu.SMEM((8, 128), i32),
            pltpu.SMEM((40, 128), i32),
            pltpu.SMEM((8, 128), f32),
        ]
        + [dma(()), dma(()), dma(()), dma((PIECES * NZ // 2,)), dma((PIECES * NZ // 2,)), dma(()), dma(())]
        + [dma((4,))] * 2
        + [dma(())] * 4
        + [dma((2,))],
        compiler_params=pltpu.CompilerParams(
            collective_id=0, has_side_effects=True, vmem_limit_bytes=62 * 1024 * 1024
        ),
    )(
        query_vecs,
        passage_vecs,
        owner_ids.T,
        local_ids.transpose(1, 2, 0).reshape(GROUPS * WIDTH, NQ),
        cand_mask,
    )
    whole = lambda shape: pl.BlockSpec(shape, lambda i: (0,) * len(shape))
    part = pl.BlockSpec((RS_CHUNK, SHARE, DIM), lambda i: (i, 0, 0))
    loss, grad_query, grad_passage = pl.pallas_call(
        finish,
        grid=(NPASS // RS_CHUNK,),
        out_shape=outs,
        in_specs=[whole((1, NQ)), whole((NQ, QT, DIM)), whole((NQ, QT, DIM)), anywhere, part],
        out_specs=[whole((1, NQ)), whole((NQ, QT, DIM)), part],
        scratch_shapes=[pltpu.VMEM((NPASS, SHARE, DIM), bf16), dma(())],
    )(loss, query_vecs, up_query, passage_vecs, up_passage)
    return (loss.reshape(NQ), grad_query, grad_passage)


def solution(mesh):
    return jax.shard_map(
        per_device,
        mesh=mesh,
        in_specs=(
            P(("pool", "rep"), None, None),
            P("pool", None, None),
            P(("pool", "rep"), None),
            P(("pool", "rep"), None, None),
            P(("pool", "rep"), None),
        ),
        out_specs=(P(("pool", "rep")), P(("pool", "rep"), None, None), P("pool", "rep", None)),
        check_vma=False,
    )
```

```python
import math

import jax
import jax.numpy as jnp
from jax import lax
from jax.experimental import pallas as pl
from jax.experimental.pallas import tpu as pltpu
from jax.sharding import PartitionSpec as P

MESH = pl.DeviceIdType.MESH
f32, bf16, i32 = jnp.float32, jnp.bfloat16, jnp.int32

TEMPER = 0.05
LOSS_SCALE = 16.0
EPSILON = 1e-06

NP = 64
NR = 4
NZ = 8
NC = NP // NZ
PIECES = 4
CAP = 2
NQ = 16
QT = 32
DIM = 128
PT = 256
NPASS = 32
GROUPS = 4
WIDTH = 4
SLOTS = NP * CAP
QUERY, GROUP_SLOTS = WIDTH, WIDTH + 1
FLAGS, FIRST = GROUP_SLOTS + GROUPS, GROUP_SLOTS + GROUPS + WIDTH
TILE = 8
NTILES = (SLOTS * WIDTH + NPASS * (TILE - 1)) // TILE
SHARE = PT // NR
RS_CHUNK = 8
UNROLL = 23
HIGH = lax.Precision.HIGHEST


def iota(shape, dim):
    return lax.broadcasted_iota(i32, shape, dim)


def hot(cond, dtype=f32):
    return jnp.where(cond, 1.0, 0.0).astype(dtype)


def index(x, bound):
    return jnp.clip(x.astype(i32), 0, bound - 1)


def dot(a, b):
    return jnp.dot(a.astype(bf16), b.astype(bf16), preferred_element_type=f32)


def dot_nt(a, b):
    return lax.dot_general(
        a.astype(bf16), b.astype(bf16), (((1,), (1,)), ((), ())), preferred_element_type=f32
    )


def hdot(a, b):
    return jnp.dot(a, b, preferred_element_type=f32, precision=HIGH)


def hdot_nt(a, b):
    return lax.dot_general(
        a, b, (((1,), (1,)), ((), ())), preferred_element_type=f32, precision=HIGH
    )


def kernel(
    q_ref, p_any, own_ref, loc_ref, mask_ref,
    loss_ref, uq_ref, up_ref,
    p_raw, p_low, q_low, plus1, plus2, plus3, minus1, minus2, minus3, far, q_send, q_recv,
    m_a, m_b, m_c, s_a, s_b, s_c,
    rows_ref, rhs_ref, soft_ref, a_ref, qn_ref, ret_send, ret_recv, rs_send, rs_recv, via_plus, via_minus, sum_plus, sum_minus,
    tbla_v, tblm_v, tblb_v, wt_v, tbla, tblm, tblb, wt,
    sem_p, sem_tbl, hop_s, plus_r, minus_r, q_ss, q_rs, m_sem, s_sem, r_ss, r_rs, x_ss, x_rs, v_rs,
):
    me = lax.axis_index("pool")
    rep = lax.axis_index("rep")
    z = lax.div(me, NC)
    c = lax.rem(me, NC)

    def wait_bytes(ref, sem):
        pltpu.make_async_copy(ref, ref, sem).wait()

    def to_pool(src, dst, ss, rs, peer):
        return pltpu.make_async_remote_copy(
            src_ref=src, dst_ref=dst, send_sem=ss, recv_sem=rs, device_id=(peer, rep), device_id_type=MESH
        )

    def along_z(e):
        return NC * lax.rem(z + NZ + e, NZ) + c

    def in_plane(e):
        return NC * z + lax.rem(c + e, NC)

    def first_hop(send, mid, sems):
        for e in range(1, NZ):
            target = lax.rem(z + e, NZ)
            to_pool(send.at[target], mid.at[z], sems.at[0], sems.at[1], NC * target + c).start()
        mid[z] = send[z]

    def second_hop(mid, recv, sems):
        wait_bytes(mid.at[pl.ds(0, NZ - 1)], sems.at[1])
        for e in range(1, NC):
            target = lax.rem(c + e, NC)
            to_pool(mid.at[:, target], recv.at[:, c], sems.at[2], sems.at[3], NC * z + target).start()
        for k in range(NZ):
            recv[k, c] = mid[k, c]

    def arrived(recv, sems):
        wait_bytes(recv.at[pl.ds(0, NC - 1)], sems.at[3])

    def put_rows(send, rows):
        for peer in range(NP):
            send[peer // NC, peer % NC] = rows[CAP * peer : CAP * (peer + 1), :]

    def take_rows(recv):
        for peer in range(NP):
            rows_ref[CAP * peer : CAP * (peer + 1), :] = recv[peer // NC, peer % NC]

    p_copy = pltpu.make_async_copy(p_any, p_raw, sem_p)
    p_copy.start()

    barrier = pltpu.get_barrier_semaphore()
    for e in range(1, NZ):
        pl.semaphore_signal(barrier, inc=1, device_id=(along_z(e), rep), device_id_type=MESH)
    for e in range(1, NC):
        pl.semaphore_signal(barrier, inc=1, device_id=(in_plane(e), rep), device_id_type=MESH)
    for d in range(1, NR):
        pl.semaphore_signal(
            barrier, inc=1, device_id=(me, lax.rem(rep + d, NR)), device_id_type=MESH
        )

    for a in range(NQ):
        x = q_ref[a].astype(f32)
        inv = lax.rsqrt(jnp.sum(x * x, axis=-1, keepdims=True) + EPSILON)
        q_low[a] = (x * inv).astype(bf16)

    npair = GROUPS * NQ
    eye = iota((NQ, NQ), 0) == iota((NQ, NQ), 1)
    own_f = own_ref[...].astype(f32)
    own_col = jnp.concatenate(
        [
            jnp.sum(jnp.where(eye, own_f[g : g + 1, :], 0.0), axis=1, keepdims=True)
            for g in range(GROUPS)
        ],
        axis=0,
    )
    loc_f = dot_nt(hot(eye), loc_ref[...].astype(f32))
    mask_f = mask_ref[...].astype(f32)
    src_r, dst_c = iota((NQ, 128), 0), iota((NQ, 128), 1)
    places = [hot((src_r == WIDTH * g + dst_c) & (dst_c < WIDTH)) for g in range(GROUPS)]
    shifted = [
        hot((src_r == WIDTH * g + dst_c - FLAGS) & (dst_c >= FLAGS) & (dst_c < FLAGS + WIDTH))
        for g in range(GROUPS)
    ]
    loc_w = jnp.concatenate([dot(loc_f, place) for place in places], axis=0)
    ra, ca = iota((npair, npair), 0), iota((npair, npair), 1)
    own_row = jnp.sum(jnp.where(ra == ca, own_col, 0.0), axis=0, keepdims=True)
    same = own_col == own_row
    rank_col = jnp.sum(hot(same & (ca % NQ < ra % NQ)), axis=1, keepdims=True)
    rank_row = jnp.sum(hot(same & (ra % NQ < ca % NQ)), axis=0, keepdims=True)
    slot_col = CAP * own_col + rank_col
    slot_row = CAP * own_row + rank_row
    st = hot(slot_col == iota((npair, SLOTS), 1).astype(f32))
    s_hot = hot(slot_row == iota((SLOTS, npair), 0).astype(f32))
    slot_wide = jnp.sum(
        jnp.where(iota((npair, 128), 0) == iota((npair, 128), 1), slot_col, 0.0),
        axis=0, keepdims=True,
    )
    tbla_v[...] = index(jnp.broadcast_to(slot_wide, (8, 128)), SLOTS)
    tbla_copy = pltpu.make_async_copy(tbla_v, tbla, sem_tbl)
    tbla_copy.start()
    lane_q = iota((NQ, 128), 1)
    group_slots = jnp.zeros((NQ, 128), f32)
    for g in range(GROUPS):
        group_slots = jnp.where(lane_q == GROUP_SLOTS + g, slot_col[NQ * g : NQ * (g + 1)], group_slots)
    flags = [dot(mask_f, place) for place in shifted]
    flags[0] = jnp.where((lane_q == FLAGS) | (lane_q == FIRST), 1.0, flags[0])
    lane_n = iota((npair, 128), 1)
    pair_rows = loc_w + jnp.concatenate([group_slots + f for f in flags], axis=0)
    pair_rows = jnp.where(lane_n == QUERY, (iota((npair, 128), 0) % NQ).astype(f32), pair_rows)
    put_rows(m_a, dot(s_hot, pair_rows))
    tbla_copy.wait()
    pl.semaphore_wait(barrier, NZ - 1 + NC - 1 + NR - 1)

    first_hop(m_a, m_b, m_sem)

    plus = [q_low, plus1, plus2, plus3, far]
    minus = [q_low, minus1, minus2, minus3, far]
    last_hop = NZ // 2 - 1
    piece = NQ // PIECES

    def pass_on(h, k):
        rows = pl.ds(piece * k, piece)
        if h < last_hop or 2 * k < PIECES:
            to_pool(
                plus[h].at[rows], plus[h + 1].at[rows], hop_s, plus_r.at[PIECES * h + k], along_z(1)
            ).start()
        if h < last_hop or 2 * k >= PIECES:
            to_pool(
                minus[h].at[rows], minus[h + 1].at[rows], hop_s, minus_r.at[PIECES * h + k], along_z(-1)
            ).start()

    def relay(h):
        for k in range(PIECES):
            rows = pl.ds(piece * k, piece)
            wait_bytes(plus[h].at[rows], plus_r.at[PIECES * (h - 1) + k])
            wait_bytes(minus[h].at[rows], minus_r.at[PIECES * (h - 1) + k])
            pass_on(h, k)

    for k in range(PIECES):
        pass_on(0, k)

    second_hop(m_b, m_c, m_sem)
    take_rows(m_b)
    r_i, c_i = iota((128, 128), 0), iota((128, 128), 1)
    picked = jnp.sum(
        jnp.where(r_i == c_i, rows_ref[:, QUERY : QUERY + 1], 0.0), axis=0, keepdims=True
    )
    tblm_v[...] = index(jnp.broadcast_to(picked, (8, 128)), NQ)
    tblm_copy = pltpu.make_async_copy(tblm_v, tblm, sem_tbl)
    tblm_copy.start()

    def deliver(block, source):
        for e in range(1, NC):
            target = lax.rem(c + e, NC)
            row = CAP * (NC * source + target)
            for k in range(CAP):
                q_send[row + k] = block[tblm[0, row + k]]
            to_pool(
                q_send.at[pl.ds(row, CAP)],
                q_recv.at[pl.ds(CAP * (NC * source + c), CAP)],
                q_ss, q_rs, NC * z + target,
            ).start()
        row = CAP * (NC * source + c)
        for k in range(CAP):
            q_recv[row + k] = block[tblm[0, row + k]]

    def deliver_both(h):
        deliver(plus[h], lax.rem(z + NZ - h, NZ))
        deliver(minus[h], lax.rem(z + h, NZ))

    def norm_passage(p, _):
        x = p_raw[p].astype(f32)
        inv = lax.rsqrt(jnp.sum(x * x, axis=-1, keepdims=True) + EPSILON)
        p_low[p] = (x * inv).astype(bf16)
        return 0

    relay(1)
    tblm_copy.wait()
    deliver(q_low, z)
    deliver_both(1)
    relay(2)
    deliver_both(2)
    relay(3)
    deliver_both(3)
    p_copy.wait()
    lax.fori_loop(0, NPASS // 2, norm_passage, 0, unroll=2)
    for k in range(PIECES):
        rows = pl.ds(piece * k, piece)
        arrival = plus_r if 2 * k < PIECES else minus_r
        wait_bytes(far.at[rows], arrival.at[PIECES * last_hop + k])
    deliver(far, lax.rem(z + NZ // 2, NZ))

    arrived(m_c, m_sem)
    take_rows(m_c)
    loc_r = rows_ref[...]
    pc, jc, pr, jr = c_i % NPASS, c_i // NPASS, r_i % NPASS, r_i // NPASS
    one_hot = hot(dot(loc_r, hot((r_i == jc) & (r_i < WIDTH))) == pc.astype(f32))
    before = dot(hot(c_i < r_i), one_hot)
    total = jnp.broadcast_to(jnp.sum(one_hot, axis=0, keepdims=True), (8, 128))
    base = dot(total, hot((pr == pc) & (jr < jc)))[0:1, :]
    tiles = jnp.floor((dot(total, hot(pr == pc)) + (TILE - 1)) * (1.0 / TILE))
    offset = dot(tiles, hot((jr == 0) & (pr < pc)))
    rank = base + before
    rank_tile = jnp.floor(rank * (1.0 / TILE))
    x_tile = one_hot * (offset[0:1, :] + rank_tile)
    x_rest = one_hot * (rank - TILE * rank_tile)
    fold = hot((c_i == jr) & (c_i < WIDTH))
    tile_c = dot(x_tile, fold)
    rest_c = dot(x_rest, fold)
    fold_row = hot(iota((8, 128), 0) == iota((8, 128), 1) // NPASS)
    tile_r = dot_nt(fold_row, x_tile)
    rest_r = dot_nt(fold_row, x_rest)
    loc_rows = dot_nt(hot(iota((8, 128), 0) == iota((8, 128), 1)), loc_r)
    slot_rows = dot_nt(hot(iota((8, 128), 0) + GROUP_SLOTS == iota((8, 128), 1)), loc_r)
    valid_c = dot(loc_r, hot((r_i == c_i + FLAGS) & (c_i < WIDTH)))
    first_row = dot_nt(hot(iota((8, 128), 1) == FIRST), loc_r)[0:1, :]
    sub8 = iota((8, 128), 0).astype(f32)
    slot_ids = iota((8, 128), 1).astype(f32)
    table = jnp.zeros((16, 128), f32)
    for j in range(WIDTH):
        rest_j = rest_r[j : j + 1, :]
        lhs = jnp.concatenate(
            [
                jnp.where(rest_j == sub8, slot_ids, 0.0),
                jnp.where(rest_j == 0.0, loc_rows[j : j + 1, :], jnp.zeros((8, 128), f32)),
            ],
            axis=0,
        )
        rhs = hot(tile_c[:, j : j + 1] == c_i.astype(f32))
        rhs_ref[j] = rhs
        table = table + dot(lhs, rhs)
    tblb_v[0:8, :] = index(table[0:8], SLOTS)
    tblb_v[8:16, :] = index(table[8:16], NPASS)
    tblb_v[16:24, :] = index(TILE * tile_r + rest_r, NTILES * TILE)
    tblb_v[24:32, :] = index(offset + tiles - 1.0, NTILES)
    tblb_v[32:40, :] = index(tiles, 2)
    tblb_copy = pltpu.make_async_copy(tblb_v, tblb, sem_tbl)
    tblb_copy.start()
    lax.fori_loop(NPASS // 2, NPASS, norm_passage, 0, unroll=2)
    tblb_copy.wait()

    wait_bytes(q_recv.at[pl.ds(0, CAP * NZ * (NC - 1))], q_rs)
    ones = jnp.ones((PT, DIM), bf16)
    lane8 = iota((8, 128), 1)

    def forward_tile(t, scores):
        p_tile = p_low[tblb[8, t]]
        q_tile = jnp.concatenate([q_recv[tblb[r, t]] for r in range(TILE)], axis=0)
        sims = lax.dot_general(
            q_tile, p_tile, (((1,), (1,)), ((), ())), preferred_element_type=f32
        )
        soft = jnp.exp2(sims * (math.log2(math.e) / TEMPER)).astype(bf16)
        soft_ref[t] = soft
        both = jnp.dot(
            soft, jnp.concatenate([p_tile, ones], axis=1), preferred_element_type=f32
        )
        sums = both[:, DIM:]
        inv = 1.0 / sums
        a_ref[pl.ds(TILE * t, TILE)] = (both[:, :DIM] * inv).reshape(TILE, QT, DIM)
        qn_ref[t] = q_tile.astype(f32) * inv
        means = (sums * (1.0 / PT)).reshape(TILE, QT // 8, 8, DIM)
        product = means[:, 0]
        for i in range(1, QT // 8):
            product = product * means[:, i]
        logs = jnp.sum(jnp.log(product), axis=1)
        score = TEMPER * (logs + QT * math.log(PT))
        return jnp.where(lane8 == t, score, scores)

    scores = lax.fori_loop(0, NTILES, forward_tile, jnp.zeros((8, 128), f32), unroll=UNROLL)

    sc = jnp.zeros((SLOTS, 128), f32)
    lane_s = iota((SLOTS, 128), 1)
    lane_r = iota((SLOTS, 8), 1).astype(f32)
    for j in range(WIDTH):
        picked = hdot_nt(rhs_ref[j], scores)
        col = jnp.sum(
            jnp.where(rest_c[:, j : j + 1] == lane_r, picked, 0.0), axis=1, keepdims=True
        )
        sc = jnp.where(lane_s == j, col, sc)
    exps = jnp.exp(sc) * valid_c
    diag = r_i == c_i
    part = jnp.sum(exps, axis=1, keepdims=True)
    s_a[0:1, :] = jnp.sum(jnp.where(diag, part, 0.0), axis=0, keepdims=True)
    s_a[1:2, :] = jnp.sum(jnp.where(diag, sc[:, 0:1], 0.0), axis=0, keepdims=True)
    for e in range(1, NZ):
        to_pool(s_a, s_b.at[z], s_sem.at[0], s_sem.at[1], along_z(e)).start()
    s_b[z] = s_a[...]
    exp_rows = hdot_nt(hot(iota((8, 128), 0) == iota((8, 128), 1)), exps)
    wait_bytes(s_b.at[pl.ds(0, NZ - 1)], s_sem.at[1])
    for e in range(1, NC):
        to_pool(s_b, s_c.at[c], s_sem.at[2], s_sem.at[3], in_plane(e)).start()
    s_c[c] = s_b[...]
    wait_bytes(s_c.at[pl.ds(0, NC - 1)], s_sem.at[3])
    for peer in range(NP):
        rows_ref[CAP * peer : CAP * (peer + 1), :] = s_c[peer % NC, peer // NC]

    sums = rows_ref[...]
    twin = jnp.where(c_i % 2 == 0, pltpu.roll(sums, 127, 1), pltpu.roll(sums, 1, 1))
    denom = jnp.zeros((1, 128), f32)
    odd_lane = (iota((1, 128), 1) % 2).astype(f32)
    for g in range(GROUPS):
        target = slot_rows[g : g + 1, :]
        odd = target - 2.0 * jnp.floor(target * 0.5)
        value = jnp.where(odd == odd_lane, sums, twin)
        denom = denom + jnp.sum(
            jnp.where(r_i.astype(f32) == target - odd, value, 0.0), axis=0, keepdims=True
        )
    denom = jnp.where(denom > 0.0, denom, 1.0)
    w_rows = LOSS_SCALE * (
        exp_rows / denom - jnp.where(iota((8, 128), 0) == 0, first_row, 0.0)
    )

    w_tile = jnp.zeros((8, 128), f32)
    for j in range(WIDTH):
        lhs = jnp.where(rest_r[j : j + 1, :] == sub8, w_rows[j : j + 1, :], 0.0)
        w_tile = w_tile + hdot(lhs, rhs_ref[j])
    wt_v[...] = w_tile
    wt_copy = pltpu.make_async_copy(wt_v, wt, sem_tbl)
    wt_copy.start()
    wt_copy.wait()

    def group_grad(s):
        acc = jnp.zeros((QT, DIM), f32)
        for j in range(WIDTH):
            pos = tblb[16 + j, s]
            acc = acc + wt[pos & (TILE - 1), pos >> 3] * a_ref[pos]
        return acc.astype(bf16)

    def send_ret(d, _):
        peer = lax.rem(me + d, NP)
        for k in range(CAP):
            ret_send[CAP * peer + k] = group_grad(CAP * peer + k)
        to_pool(
            ret_send.at[pl.ds(CAP * peer, CAP)], ret_recv.at[pl.ds(CAP * me, CAP)], r_ss, r_rs, peer
        ).start()
        return 0

    lax.fori_loop(1, NP, send_ret, 0)
    for k in range(CAP):
        ret_recv[CAP * me + k] = group_grad(CAP * me + k)

    odd = slot_col - 2.0 * jnp.floor(slot_col * 0.5)
    own_rows = [
        jnp.sum(
            jnp.where(
                diag,
                jnp.sum(jnp.where(c_i == CAP * me + k, sums, 0.0), axis=1, keepdims=True),
                0.0,
            ),
            axis=0, keepdims=True,
        )
        for k in range(CAP)
    ]
    own = jnp.where(odd == 0.0, own_rows[0], own_rows[1])
    lane_f = iota((npair, 128), 1).astype(f32)
    pair_sum = jnp.sum(jnp.where(lane_f == slot_col - odd, own, 0.0), axis=1, keepdims=True)
    pair_score = jnp.sum(jnp.where(lane_f == slot_col - odd + 1.0, own, 0.0), axis=1, keepdims=True)
    total_sum = pair_sum[0:NQ]
    for g in range(1, GROUPS):
        total_sum = total_sum + pair_sum[NQ * g : NQ * (g + 1)]
    losses = jnp.log(total_sum) - pair_score[0:NQ]
    loss_ref[...] = jnp.sum(jnp.where(eye, losses, 0.0), axis=0, keepdims=True)

    def passage_tile(t, acc):
        qs = jnp.concatenate(
            [
                (qn_ref[t, QT * r : QT * (r + 1), :] * wt[r, t]).astype(bf16)
                for r in range(TILE)
            ],
            axis=0,
        )
        grad = lax.dot_general(
            qs, soft_ref[t], (((0,), (0,)), ((), ())), preferred_element_type=f32
        )
        halves = jnp.concatenate([grad[:, :128], grad[:, 128:]], axis=0)
        prev = jnp.maximum(t - 1, 0)
        again = (t > 0) & (tblb[8, t] == tblb[8, prev])
        keep = jnp.where(again, 1.0, 0.0).astype(f32)
        acc = halves + keep * acc
        a_ref[pl.ds(TILE * t, TILE)] = acc.reshape(TILE, QT, DIM)
        return acc

    lax.fori_loop(0, NTILES, passage_tile, jnp.zeros((PT, DIM), f32), unroll=UNROLL)

    after, opposite, before_me = (lax.rem(rep + d, NR) for d in (1, 2, 3))

    def to_rep(src, dst, rs, target):
        pltpu.make_async_remote_copy(
            src_ref=src, dst_ref=dst, send_sem=x_ss, recv_sem=rs, device_id=(me, target), device_id_type=MESH
        ).start()

    for chunk in range(NPASS // RS_CHUNK):

        def cut_passage(i, _):
            p = chunk * RS_CHUNK + i
            last = TILE * tblb[24, p]
            used = tblb[32, p].astype(f32)
            for half in range(2):
                x = jnp.concatenate(
                    [a_ref[last + 4 * half + m] for m in range(4)], axis=0
                )
                y = (x * used).T.astype(bf16)
                for part in range(2):
                    rs_send[2 * half + part, p] = y[SHARE * part : SHARE * (part + 1), :]
            return 0

        lax.fori_loop(0, RS_CHUNK, cut_passage, 0, unroll=RS_CHUNK)
        rows = pl.ds(chunk * RS_CHUNK, RS_CHUNK)
        if 2 * chunk * RS_CHUNK < NPASS:
            to_rep(rs_send.at[opposite, rows], via_plus.at[rows], v_rs.at[0], after)
            to_rep(rs_send.at[before_me, rows], rs_recv.at[1, rows], x_rs, before_me)
        else:
            back = pl.ds(chunk * RS_CHUNK - NPASS // 2, RS_CHUNK)
            to_rep(rs_send.at[opposite, rows], via_minus.at[back], v_rs.at[1], before_me)
            to_rep(rs_send.at[after, rows], rs_recv.at[0, rows], x_rs, after)

    low, top = pl.ds(0, NPASS // 2), pl.ds(NPASS // 2, NPASS // 2)
    wait_bytes(via_plus, v_rs.at[0])

    def add_plus(i, _):
        sum_plus[i] = (rs_send[after, i].astype(f32) + via_plus[i].astype(f32)).astype(bf16)
        return 0

    lax.fori_loop(0, NPASS // 2, add_plus, 0, unroll=4)
    to_rep(sum_plus, rs_recv.at[0, low], x_rs, after)
    wait_bytes(via_minus, v_rs.at[1])

    def add_minus(i, _):
        sum_minus[i] = (
            rs_send[before_me, NPASS // 2 + i].astype(f32) + via_minus[i].astype(f32)
        ).astype(bf16)
        return 0

    lax.fori_loop(0, NPASS // 2, add_minus, 0, unroll=4)
    to_rep(sum_minus, rs_recv.at[1, top], x_rs, before_me)

    wait_bytes(ret_recv.at[pl.ds(0, CAP * (NP - 1))], r_rs)

    def sum_query(a, _):
        up = jnp.zeros((QT, DIM), f32)
        for g in range(GROUPS):
            up = up + ret_recv[tbla[0, NQ * g + a]].astype(f32)
        uq_ref[a] = up
        return 0

    lax.fori_loop(0, NQ, sum_query, 0, unroll=4)

    wait_bytes(rs_recv, x_rs)

    def sum_passage(p, _):
        up = rs_send[rep, p].astype(f32)
        for d in range(2):
            up = up + rs_recv[d, p].astype(f32)
        up_ref[p] = up
        return 0

    lax.fori_loop(0, NPASS, sum_passage, 0, unroll=4)

    wait_bytes(m_a.at[pl.ds(0, NZ - 1)], m_sem.at[0])
    wait_bytes(m_a.at[pl.ds(0, NC - 1)], m_sem.at[2])
    wait_bytes(s_b.at[pl.ds(0, NZ - 1)], s_sem.at[0])
    wait_bytes(s_c.at[pl.ds(0, NC - 1)], s_sem.at[2])
    wait_bytes(q_send.at[pl.ds(0, NQ * (NZ - 1))], hop_s)
    wait_bytes(q_send.at[pl.ds(0, CAP * NZ * (NC - 1))], q_ss)
    wait_bytes(ret_send.at[pl.ds(0, CAP * (NP - 1))], r_ss)
    wait_bytes(rs_send.at[pl.ds(0, NR - 1)], x_ss)


def unit_backward(x, up):
    x = x.astype(f32)
    inv = lax.rsqrt(jnp.sum(x * x, axis=-1, keepdims=True) + EPSILON)
    unit = x * inv
    return inv * (up - unit * jnp.sum(unit * up, axis=-1, keepdims=True))


def finish(loss_in, q_ref, uq_ref, p_any, up_ref, loss_ref, gq_ref, gp_ref, p_share, sem):
    step = pl.program_id(0)

    @pl.when(step == 0)
    def _():
        start = pl.multiple_of(lax.axis_index("rep") * SHARE, SHARE)
        copy = pltpu.make_async_copy(p_any.at[:, pl.ds(start, SHARE)], p_share, sem)
        copy.start()
        loss_ref[...] = loss_in[...]
        for a in range(NQ):
            gq_ref[a] = unit_backward(q_ref[a], uq_ref[a])
        copy.wait()

    for i in range(RS_CHUNK):
        gp_ref[i] = unit_backward(p_share[step * RS_CHUNK + i], up_ref[i])


def per_device(query_vecs, passage_vecs, owner_ids, local_ids, cand_mask):
    vmem = pl.BlockSpec(memory_space=pltpu.VMEM)
    anywhere = pl.BlockSpec(memory_space=pl.ANY)
    rows = pltpu.VMEM((NZ, NC, CAP, 128), f32)
    block = pltpu.VMEM((NQ, QT, DIM), bf16)
    dma = pltpu.SemaphoreType.DMA
    outs = (
        jax.ShapeDtypeStruct((1, NQ), f32),
        jax.ShapeDtypeStruct((NQ, QT, DIM), f32),
        jax.ShapeDtypeStruct((NPASS, SHARE, DIM), f32),
    )
    loss, up_query, up_passage = pl.pallas_call(
        kernel,
        out_shape=outs,
        in_specs=[vmem, anywhere, vmem, vmem, vmem],
        out_specs=[vmem, vmem, vmem],
        scratch_shapes=[
            pltpu.VMEM((NPASS, PT, DIM), bf16),
            pltpu.VMEM((NPASS, PT, DIM), bf16),
        ]
        + [block] * 8
        + [
            pltpu.VMEM((SLOTS, QT, DIM), bf16),
            pltpu.VMEM((SLOTS, QT, DIM), bf16),
        ]
        + [rows] * 3
        + [
            pltpu.VMEM((CAP, 128), f32),
            pltpu.VMEM((NZ, CAP, 128), f32),
            pltpu.VMEM((NC, NZ, CAP, 128), f32),
            pltpu.VMEM((SLOTS, 128), f32),
            pltpu.VMEM((WIDTH, 128, 128), f32),
            pltpu.VMEM((NTILES, TILE * QT, PT), bf16),
            pltpu.VMEM((NTILES * TILE, QT, DIM), f32),
            pltpu.VMEM((NTILES, TILE * QT, DIM), f32),
            pltpu.VMEM((SLOTS, QT, DIM), bf16),
            pltpu.VMEM((SLOTS, QT, DIM), bf16),
            pltpu.VMEM((NR, NPASS, SHARE, DIM), bf16),
            pltpu.VMEM((2, NPASS, SHARE, DIM), bf16),
        ]
        + [pltpu.VMEM((NPASS // 2, SHARE, DIM), bf16)] * 4
        + [
            pltpu.VMEM((8, 128), i32),
            pltpu.VMEM((8, 128), i32),
            pltpu.VMEM((40, 128), i32),
            pltpu.VMEM((8, 128), f32),
            pltpu.SMEM((8, 128), i32),
            pltpu.SMEM((8, 128), i32),
            pltpu.SMEM((40, 128), i32),
            pltpu.SMEM((8, 128), f32),
        ]
        + [dma(()), dma(()), dma(()), dma((PIECES * NZ // 2,)), dma((PIECES * NZ // 2,)), dma(()), dma(())]
        + [dma((4,))] * 2
        + [dma(())] * 4
        + [dma((2,))],
        compiler_params=pltpu.CompilerParams(
            collective_id=0, has_side_effects=True, vmem_limit_bytes=62 * 1024 * 1024
        ),
    )(
        query_vecs,
        passage_vecs,
        owner_ids.T,
        local_ids.transpose(1, 2, 0).reshape(GROUPS * WIDTH, NQ),
        cand_mask,
    )
    whole = lambda shape: pl.BlockSpec(shape, lambda i: (0,) * len(shape))
    part = pl.BlockSpec((RS_CHUNK, SHARE, DIM), lambda i: (i, 0, 0))
    loss, grad_query, grad_passage = pl.pallas_call(
        finish,
        grid=(NPASS // RS_CHUNK,),
        out_shape=outs,
        in_specs=[whole((1, NQ)), whole((NQ, QT, DIM)), whole((NQ, QT, DIM)), anywhere, part],
        out_specs=[whole((1, NQ)), whole((NQ, QT, DIM)), part],
        scratch_shapes=[pltpu.VMEM((NPASS, SHARE, DIM), bf16), dma(())],
    )(loss, query_vecs, up_query, passage_vecs, up_passage)
    return (loss.reshape(NQ), grad_query, grad_passage)


def solution(mesh):
    return jax.shard_map(
        per_device,
        mesh=mesh,
        in_specs=(
            P(("pool", "rep"), None, None),
            P("pool", None, None),
            P(("pool", "rep"), None),
            P(("pool", "rep"), None, None),
            P(("pool", "rep"), None),
        ),
        out_specs=(P(("pool", "rep")), P(("pool", "rep"), None, None), P("pool", "rep", None)),
        check_vma=False,
    )
```
